128 devices in a mesh: ctx: 16 (over y, x_hi, core), exp: 8 (over x_lo, z).
Axes of the slice: x: 4 (x_hi: 2, x_lo: 2; x = x_hi * 2 + x_lo), y: 4, z: 4, core: 2. Of those that a mesh axis runs over, the one named last changes fastest.
Arguments:
- stream: bfloat16 [2048, 4096], P(('ctx', 'exp')), may hold values from -3 to 3
- queries: bfloat16 [2048, 4096], P('ctx', 'exp'), may hold values from -108 to 108
- attn_keys: bfloat16 [2048, 1024], P('ctx', 'exp'), may hold values from -3 to 3
- attn_values: bfloat16 [2048, 1024], P('ctx', 'exp'), may hold values from -6 to 6
- out_weight: bfloat16 [4096, 4096], P('exp'), may hold values from -0.09375 to 0.09375
- norm_gain: float32 [4096], replicated, may hold values from 0.25 to 1.75
- expert_ids: int32 [2048, 2], P(('ctx', 'exp')), may hold values from 0 to 7, all different within a row; in each aligned block of 16 rows (0 to 15, 16 to 31, ...) at most 8 rows name the same one
- combine: float32 [2048, 2], P(('ctx', 'exp')), may hold values from 0.1 to 0.9
- w_gate: bfloat16 [8, 4096, 14336], P('exp', None, 'ctx'), may hold values from -0.09375 to 0.09375
- w_up: bfloat16 [8, 4096, 14336], P('exp', None, 'ctx'), may hold values from -0.09375 to 0.09375
- w_down: bfloat16 [8, 14336, 4096], P('exp', 'ctx'), may hold values from -0.046875 to 0.046875
Outputs:
- layer_out: bfloat16 [2048, 4096], P(('ctx', 'exp'))
The draws below stay inside these ranges and needn't reach their ends.
Inputs may be any that keep to these rules, and one draw needn't show every extreme that they name: `expert_ids`: taking the rows in aligned blocks of 16 (the rows of one device), no expert is named by more than 8 rows of a block, and in every draw some block names some expert exactly 8 times. The 2 experts of a row differ.
All inputs are finite; a program needn't handle non-finite values.
Results may differ from the reference program's by a relative error of at most 0.015.
Values may be sent and summed in bfloat16 or wider, within the bound.
A program may use at most 128 MiB of HBM per device.

```python
import math
import jax
import jax.numpy as jnp
import numpy as np
from jax import lax

D = 4096
HEADS = 32
KV_HEADS = 8
HEAD_DIM = 128
FF = 14336
TOP = 2
GROUP = 4
EXPERTS = 8
SEQ = 2048
TOK_ROWS = 16
CAP = 8


def joint_draw(key):
    query_key = jax.random.fold_in(key, 11)
    keys_key = jax.random.fold_in(key, 12)
    keys_field = jnp.clip(jax.random.normal(keys_key, (SEQ, KV_HEADS * HEAD_DIM), jnp.float32), -3.0, 3.0)
    query_field = jnp.clip(2.5 * jax.random.normal(query_key, (SEQ, HEADS * HEAD_DIM), jnp.float32), -10.0, 10.0)
    return (query_field, keys_field)


def draw_queries(key, part):
    return joint_draw(key)[0].astype(jnp.bfloat16)


def draw_attn_keys(key, part):
    return joint_draw(key)[1].astype(jnp.bfloat16)


def level_of(key, shape, split, least, top_value):
    loudness, own = 1.0, jax.random.fold_in(key, 6)
    for dim, parts in split:
        steps = jnp.exp(jax.random.uniform(jax.random.fold_in(own, dim), (parts,), jnp.float32, least / len(split), top_value / len(split)))
        loudness = loudness * jnp.repeat(steps, shape[dim] // parts).reshape([-1 if axis == dim else 1 for axis in range(len(shape))])
    return loudness


def assign_block(rng, own, number, rows, number_of, top, reach, slope):
    order = jax.random.permutation(rng, number_of)
    crowded, ordinary = load_shares(number_of, rows * top, reach, slope, True), load_shares(number_of, rows * top, reach, slope, False)
    places = jnp.arange(number_of)

    def named(tallies, turn):
        used = int((tallies > 0).sum())
        fixed = max(1, used // 4)
        shifted = fixed + (places - fixed + turn * (used - fixed)) % max(1, number_of - fixed)
        return jnp.zeros((number_of,), jnp.int32).at[order[jnp.where(places < fixed, places, shifted)]].set(jnp.asarray(tallies, jnp.int32))

    tallies = jnp.where(number % 4 == 0, named(crowded, number // 4), named(ordinary, number - number // 4 - 1))
    mixed = jax.random.permutation(jax.random.fold_in(own, 3), number_of)
    giver, sink = mixed[0:number_of // 2 * 2:2], mixed[1:number_of // 2 * 2:2]
    slack = jnp.minimum(tallies[giver] - 1, reach - tallies[sink]) // 2
    slack = jnp.where((giver == order[0]) | (sink == order[0]) | (tallies[sink] == 0), 0, jnp.maximum(slack, 0))
    shifted = jax.random.randint(jax.random.fold_in(own, 4), (number_of // 2,), 0, 1 << 20) % (slack + 1)
    tallies = tallies.at[giver].add(-shifted).at[sink].add(shifted)
    items = jnp.searchsorted(jnp.cumsum(tallies), jnp.arange(rows * top), side="right").astype(jnp.int32)
    grid = items.reshape(top, rows).T
    grid = grid[jax.random.permutation(jax.random.fold_in(own, 1), rows)]
    turn = jax.random.randint(jax.random.fold_in(own, 2), (rows, 1), 0, top)
    return jnp.take_along_axis(grid, (jnp.arange(top)[None, :] + turn) % top, axis=1)


def load_shares(count, total, reach, slope, full):
    portions = [(1 << 20) // math.isqrt(standing ** slope) + 1 for standing in range(1, count + 1)]
    largest = reach if full else min(reach, max(-(-total // count), total * portions[0] // sum(portions)))
    least = 1 if total - largest >= count - 1 else 0
    given, spare = [largest] + [least] * (count - 1), total - largest - least * (count - 1)
    while spare > 0:
        movable = [i for i in range(1, count) if given[i] < largest] or [i for i in range(1, count) if given[i] < reach]
        mass, remaining = sum([portions[i] for i in movable]), spare
        for i in movable:
            extra = min(reach - given[i], max(1, remaining * portions[i] // mass), spare)
            given[i] = given[i] + extra
            spare = spare - extra
    return np.array(given)


def noise(stream_key, dims, spread, bound, shards=(), held_as=jnp.bfloat16):
    array = spread * jax.random.normal(stream_key, dims, jnp.float32)
    if shards:
        array = array * level_of(stream_key, dims, shards, -0.22, 0.18)
    return jnp.clip(array, -bound, bound).astype(held_as)


def setup_inputs(seed: int = 0) -> dict:
    splits = jax.random.split(jax.random.key(seed), 12)
    stream = noise(splits[0], (SEQ, D), 0.5, 3.0, ((0, 128),))
    queries = draw_queries(jax.random.fold_in(splits[11], 71), 0)
    attn_keys = draw_attn_keys(jax.random.fold_in(splits[11], 71), 0)
    attn_values = noise(splits[3], (SEQ, KV_HEADS * HEAD_DIM), 1.0, 6.0, ((0, 16), (1, 8)))
    out_weight = noise(splits[4], (HEADS * HEAD_DIM, D), (HEADS * HEAD_DIM) ** -0.5, 0.09375, ((0, 8),))
    norm_gain = jnp.clip(1.0 + 0.15 * jax.random.normal(splits[5], (D,), jnp.float32), 0.25, 1.75)
    expert_ids_keys = jax.random.split(jax.random.fold_in(splits[6], 1), SEQ // TOK_ROWS)
    expert_ids_turns = jax.random.permutation(jax.random.fold_in(splits[6], 3), SEQ // TOK_ROWS)
    expert_ids = jax.vmap(lambda own, number: assign_block(jax.random.fold_in(splits[6], 2), own, number, TOK_ROWS, EXPERTS, TOP, CAP, 2))(expert_ids_keys, expert_ids_turns).reshape((SEQ, TOP))
    combine = jnp.clip(0.1 + 0.79999997 * jax.random.uniform(splits[7], (SEQ, TOP), jnp.float32) ** level_of(splits[7], (SEQ, TOP), ((0, 128),), -0.2, 0.2), 0.1, 0.9)
    w_gate = noise(splits[8], (EXPERTS, D, FF), D ** -0.5, 0.09375, ((0, 8), (2, 16)))
    w_up = noise(splits[9], (EXPERTS, D, FF), D ** -0.5, 0.09375, ((0, 8), (2, 16)))
    w_down = noise(splits[10], (EXPERTS, FF, D), FF ** -0.5, 0.046875, ((0, 8), (1, 16)))
    return dict(stream=stream, queries=queries, attn_keys=attn_keys, attn_values=attn_values, out_weight=out_weight, norm_gain=norm_gain, expert_ids=expert_ids, combine=combine, w_gate=w_gate, w_up=w_up, w_down=w_down)


block_rows = 128
neg_big = -1e+30

def head_attention(operands):
    query_group, key_head, value_head = operands
    positions = jnp.arange(SEQ, dtype=jnp.int32)
    allowed = positions[:, None] >= positions[None, :]
    scores = jnp.einsum('tgd,ud->gtu', query_group.astype(jnp.float32), key_head.astype(jnp.float32)) * (1.0 / math.sqrt(HEAD_DIM))
    scores = jnp.where(allowed, scores, neg_big)
    row_max = lax.optimization_barrier(jnp.max(scores, axis=-1, keepdims=True))
    weights = jnp.where(allowed, jnp.exp(scores - row_max), 0.0)
    row_total = lax.optimization_barrier(jnp.sum(weights, axis=-1))
    weight_bf = weights.astype(jnp.bfloat16)
    numerator = jnp.einsum('gtu,ud->tgd', weight_bf.astype(jnp.float32), value_head.astype(jnp.float32))
    return numerator / jnp.transpose(row_total)[..., None]

def reference(stream, queries, attn_keys, attn_values, out_weight, norm_gain, expert_ids, combine, w_gate, w_up, w_down):
    query_heads = jnp.transpose(queries.reshape(SEQ, KV_HEADS, GROUP, HEAD_DIM), (1, 0, 2, 3))
    key_heads = jnp.transpose(attn_keys.reshape(SEQ, KV_HEADS, HEAD_DIM), (1, 0, 2))
    value_heads = jnp.transpose(attn_values.reshape(SEQ, KV_HEADS, HEAD_DIM), (1, 0, 2))
    per_head = lax.map(head_attention, (query_heads, key_heads, value_heads))
    attention = jnp.transpose(per_head, (1, 0, 2, 3)).reshape(SEQ, HEADS * HEAD_DIM).astype(jnp.bfloat16)
    mixed = stream.astype(jnp.float32) + jnp.dot(attention, out_weight, preferred_element_type=jnp.float32)
    mean_square = lax.optimization_barrier(jnp.mean(mixed * mixed, axis=-1, keepdims=True))
    normed = (mixed * lax.rsqrt(mean_square + 1e-05) * norm_gain).astype(jnp.bfloat16)
    total_assign = SEQ * TOP
    flat_ids = expert_ids.reshape(total_assign).astype(jnp.int32)
    token_of = jnp.arange(total_assign, dtype=jnp.int32) // TOP
    onehot = (flat_ids[:, None] == jnp.arange(EXPERTS, dtype=jnp.int32)[None, :]).astype(jnp.int32)
    counts = lax.optimization_barrier(jnp.sum(onehot, axis=0)).astype(jnp.int32)
    slot_rank = lax.optimization_barrier(jnp.sum((jnp.cumsum(onehot, axis=0).astype(jnp.int32) - onehot) * onehot, axis=1)).astype(jnp.int32)
    padded = (counts + block_rows - 1) // block_rows * block_rows
    range_ends = jnp.cumsum(padded).astype(jnp.int32)
    range_begins = range_ends - padded
    dest_row = (range_begins[flat_ids] + slot_rank).astype(jnp.int32)
    n_blocks = (total_assign + block_rows - 1) // block_rows + EXPERTS
    row_token = jnp.zeros((n_blocks * block_rows,), jnp.int32).at[dest_row].set(token_of)
    block_first = jnp.arange(n_blocks, dtype=jnp.int32) * block_rows
    block_expert = jnp.minimum(lax.optimization_barrier(jnp.sum((range_ends[None, :] <= block_first[:, None]).astype(jnp.int32), axis=1)), EXPERTS - 1).astype(jnp.int32)

    def run_block(block_index):
        tokens_here = lax.dynamic_slice_in_dim(row_token, (block_index * block_rows).astype(jnp.int32), block_rows, 0)
        rows_here = jnp.take(normed, tokens_here, axis=0)
        expert_here = block_expert[block_index]
        gate_part = jnp.dot(rows_here, w_gate[expert_here], preferred_element_type=jnp.float32)
        up_part = jnp.dot(rows_here, w_up[expert_here], preferred_element_type=jnp.float32)
        hidden = (jax.nn.silu(gate_part) * up_part).astype(jnp.bfloat16)
        return jnp.dot(hidden, w_down[expert_here], preferred_element_type=jnp.float32).astype(jnp.bfloat16)
    expert_rows = lax.map(run_block, jnp.arange(n_blocks, dtype=jnp.int32)).reshape(n_blocks * block_rows, D)
    expert_out = jnp.take(expert_rows, dest_row, axis=0).reshape(SEQ, TOP, D).astype(jnp.float32)
    layer_out = (mixed + lax.optimization_barrier(jnp.sum(combine[..., None] * expert_out, axis=1))).astype(jnp.bfloat16)
    return layer_out
```

```python
import functools
import math

import jax
import jax.numpy as jnp
from jax import lax
from jax.experimental import pallas as pl
from jax.experimental.pallas import tpu as pltpu
from jax.sharding import PartitionSpec as P

HD = 128
MESH = pl.DeviceIdType.MESH
NEG = -1e30
F32 = jnp.float32
BF = jnp.bfloat16
NT = (((1,), (1,)), ((), ()))
TN = (((0,), (0,)), ((), ()))


def layer_kernel(
    n_ctx,
    n_exp,
    q_ref,
    k_ref,
    v_ref,
    stream_ref,
    gain_ref,
    ids_ref,
    comb_ref,
    ow_hbm,
    wg_hbm,
    wu_hbm,
    wd_hbm,
    out_ref,
    k_all,
    v_all,
    m_s,
    l_s,
    acc_s,
    att_s,
    ow_v,
    wgu_v,
    wd_v,
    ps_v,
    pr_v,
    mixed_v,
    normed_v,
    pk_v,
    a2_v,
    rows_v,
    h_v,
    part_v,
    sib_v,
    rsb_v,
    ret_v,
    w_sem,
    kv_ss,
    kv_rs,
    ps_ss,
    ps_rs,
    a_ss,
    a_rs,
    ag_ss,
    ag_rs,
    fw_ss,
    fw_rs,
    sb_ss,
    sb_rs,
    ch_ss,
    ch_rs,
    r_ss,
    r_rs,
):
    c = lax.axis_index("ctx")
    e = lax.axis_index("exp")
    span = q_ref.shape[0]
    heads = q_ref.shape[1] // HD
    toks, dim = stream_ref.shape
    cap = pk_v.shape[1]
    slots = n_exp * cap
    n_chip = n_ctx // 2
    core = lax.rem(c, 2)
    chip = c // 2
    y = c // 4
    sibling = chip * 2 + 1 - core
    n_y = n_ctx // 4
    nt = wgu_v.shape[0]
    n_ps = ps_v.shape[0]
    ps_cols = ps_v.shape[3]

    def remote(src, dst, ss, rs, tc, te):
        return pltpu.make_async_remote_copy(
            src_ref=src, dst_ref=dst, send_sem=ss, recv_sem=rs, device_id=(tc, te), device_id_type=MESH
        )

    def weight_copies(n):
        cols = pl.ds(pl.multiple_of(n * HD, HD), HD)
        return (
            pltpu.make_async_copy(wg_hbm.at[:, cols], wgu_v.at[n, :, pl.ds(0, HD)], w_sem.at[0, n]),
            pltpu.make_async_copy(wu_hbm.at[:, cols], wgu_v.at[n, :, pl.ds(HD, HD)], w_sem.at[1, n]),
        )

    ow_copy = pltpu.make_async_copy(ow_hbm, ow_v, w_sem.at[2, 0])
    wd_copy = pltpu.make_async_copy(wd_hbm, wd_v, w_sem.at[2, 1])
    ow_copy.start()

    barrier = pltpu.get_barrier_semaphore()

    @pl.loop(1, n_ctx)
    def _(d):
        pl.semaphore_signal(barrier, inc=1, device_id=(lax.rem(c + d, n_ctx), e), device_id_type=MESH)

    @pl.loop(1, n_exp)
    def _(d):
        pl.semaphore_signal(barrier, inc=1, device_id=(c, lax.rem(e + d, n_exp)), device_id_type=MESH)

    pl.semaphore_wait(barrier, n_ctx - 1 + n_exp - 1)

    def kv_pair(j, src_block):
        return (
            remote(k_ref, k_all.at[src_block], kv_ss.at[0, j], kv_rs.at[0, src_block], j, e),
            remote(v_ref, v_all.at[src_block], kv_ss.at[1, j], kv_rs.at[1, src_block], j, e),
        )

    @pl.loop(c + 1, n_ctx)
    def _(j):
        for cp in kv_pair(j, c):
            cp.start()

    @pl.loop(0, nt)
    def _(n):
        for cp in weight_copies(n):
            cp.start()

    wd_copy.start()

    k_all[c] = k_ref[...]
    v_all[c] = v_ref[...]
    last_group = c // 4

    @pl.loop(c + 1, last_group * 4 + 4)
    def _(j):
        k_all[j] = jnp.zeros(k_ref.shape, BF)
        v_all[j] = jnp.zeros(v_ref.shape, BF)

    m_s[...] = jnp.full(m_s.shape, NEG, F32)
    l_s[...] = jnp.zeros(l_s.shape, F32)
    acc_s[...] = jnp.zeros(acc_s.shape, F32)
    scale = 1.0 / math.sqrt(HD)

    @pl.loop(0, last_group + 1)
    def _(g):
        @pl.loop(g * 4, jnp.minimum(g * 4 + 4, c))
        def _(j):
            for cp in kv_pair(c, j):
                cp.wait_recv()

        keys = k_all[pl.ds(g * 4, 4)].reshape(4 * span, HD)
        vals = v_all[pl.ds(g * 4, 4)].reshape(4 * span, HD)
        row = lax.broadcasted_iota(jnp.int32, (span, 4 * span), 0) + (c - g * 4) * span
        col = lax.broadcasted_iota(jnp.int32, (span, 4 * span), 1)
        allowed = row >= col
        for h in range(heads):
            s = lax.dot_general(q_ref[:, h * HD : (h + 1) * HD], keys, NT, preferred_element_type=F32) * scale
            s = jnp.where(allowed, s, NEG)
            m_old = m_s[h]
            m_new = jnp.maximum(m_old, jnp.max(s, axis=1, keepdims=True))
            p = jnp.exp(s - m_new[:, :1])
            fix = jnp.exp(m_old - m_new)
            l_s[h] = l_s[h] * fix + jnp.sum(p, axis=1, keepdims=True)
            acc_s[h] = acc_s[h] * fix + jnp.dot(p.astype(BF), vals, preferred_element_type=F32)
            m_s[h] = m_new

    for h in range(heads):
        att_s[:, h * HD : (h + 1) * HD] = (acc_s[h] / l_s[h]).astype(BF)

    ow_copy.wait()

    def ps_copy(n, te, src_e):
        return remote(ps_v.at[n, te], pr_v.at[n, src_e], ps_ss.at[n, te], ps_rs.at[n, src_e], c, te)

    @pl.loop(0, n_ps)
    def _(n):
        cols = pl.ds(pl.multiple_of(n * ps_cols, ps_cols), ps_cols)
        r = jnp.dot(att_s[...], ow_v[:, cols], preferred_element_type=F32)
        ps_v[n] = r.reshape(n_exp, toks, ps_cols).astype(BF)

        @pl.loop(1, n_exp)
        def _(d):
            ps_copy(n, lax.rem(e + d, n_exp), e).start()

        pr_v[n, e] = ps_v[n, e]

    @pl.loop(0, n_ps)
    def _(n):
        @pl.loop(1, n_exp)
        def _(d):
            ps_copy(n, e, lax.rem(e + d, n_exp)).wait_recv()

        cols = pl.ds(pl.multiple_of(n * ps_cols, ps_cols), ps_cols)
        total = jnp.sum(pr_v[n].astype(F32), axis=0)
        mixed_v[:, cols] = stream_ref[:, cols].astype(F32) + total

    mixed = mixed_v[...]
    mean_sq = jnp.mean(mixed * mixed, axis=1, keepdims=True)
    normed_v[...] = (mixed * lax.rsqrt(mean_sq + 1e-05) * gain_ref[...]).astype(BF)

    slot_row = lax.broadcasted_iota(jnp.int32, (slots, toks), 0)
    slot_exp = slot_row // cap
    first = ids_ref[0:1, :] == slot_exp
    second = ids_ref[1:2, :] == slot_exp
    named = jnp.where(first | second, 1.0, 0.0)
    tri = jnp.where(
        lax.broadcasted_iota(jnp.int32, (toks, toks), 0) < lax.broadcasted_iota(jnp.int32, (toks, toks), 1), 1.0, 0.0
    )
    rank = jnp.dot(named.astype(BF), tri.astype(BF), preferred_element_type=F32)
    slot_rank = (slot_row - slot_exp * cap).astype(F32)
    chosen = jnp.where(rank == slot_rank, named, 0.0)

    blk = 512

    @pl.loop(0, dim // blk)
    def _(j):
        cols = pl.ds(pl.multiple_of(j * blk, blk), blk)
        r = jnp.dot(chosen.astype(BF), normed_v[:, cols], preferred_element_type=F32)
        pk_v[:, :, cols] = r.reshape(n_exp, cap, blk).astype(BF)

    def a_copy(te, src_e):
        return remote(pk_v.at[te], a2_v.at[src_e], a_ss.at[te], a_rs.at[src_e], c, te)

    @pl.loop(1, n_exp)
    def _(d):
        a_copy(lax.rem(e + d, n_exp), e).start()

    a2_v[e] = pk_v[e]

    @pl.loop(1, n_exp)
    def _(d):
        a_copy(e, lax.rem(e + d, n_exp)).wait_recv()

    @pl.loop(0, dim // blk)
    def _(j):
        cols = pl.ds(pl.multiple_of(j * blk, blk), blk)
        rows_v[c, :, cols] = a2_v[:, :, cols].astype(F32).reshape(slots, blk).astype(BF)

    def ag_copy(to_chip, src_chip):
        b = src_chip * 2 + core
        return remote(rows_v.at[b], rows_v.at[b], ag_ss.at[to_chip], ag_rs.at[src_chip], to_chip * 2 + core, e)

    def fw_copy(src_chip, src_core):
        b = src_chip * 2 + src_core
        return remote(rows_v.at[b], rows_v.at[b], fw_ss.at[src_chip], fw_rs.at[src_chip], sibling, e)

    def step_off(s):
        return s ^ (s // 2)

    fw_copy(chip, core).start()

    xh = lax.rem(chip, 2)
    partner = chip + 1 - 2 * xh
    ag_copy(partner, chip).start()

    @pl.loop(1, n_y)
    def _(s):
        ty = lax.rem(y + n_y - step_off(s), n_y)
        ag_copy(ty * 2 + xh, chip).start()
        ag_copy(ty * 2 + 1 - xh, chip).start()

    ag_copy(chip, partner).wait_recv()
    fw_copy(partner, core).start()

    @pl.loop(0, nt)
    def _(n):
        for cp in weight_copies(n):
            cp.wait()

    wd_copy.wait()

    def sb_copy(q, of_core):
        return remote(part_v.at[q * 2 + of_core], sib_v.at[q], sb_ss.at[q], sb_rs.at[q], sibling, e)

    def ch_copy(to_chip, src_chip):
        return remote(
            part_v.at[to_chip * 2 + core],
            rsb_v.at[src_chip],
            ch_ss.at[to_chip],
            ch_rs.at[src_chip],
            to_chip * 2 + core,
            e,
        )

    def finish(yy):
        for x2 in range(2):
            q = yy * 2 + x2
            sb_copy(q, core).wait_recv()
            b = q * 2 + core

            @pl.loop(0, dim // blk)
            def _(j):
                cols = pl.ds(pl.multiple_of(j * blk, blk), blk)
                part_v[b, :, cols] = (part_v[b, :, cols].astype(F32) + sib_v[q, :, cols].astype(F32)).astype(BF)

            @pl.when(q != chip)
            def _():
                ch_copy(q, chip).start()

    rows_chunk = 4 * slots

    @pl.loop(0, n_y)
    def _(s):
        yy = lax.rem(y + step_off(s), n_y)
        for x2 in range(2):
            fw_copy(yy * 2 + x2, 1 - core).wait_recv()

        @pl.loop(0, nt)
        def _(n):
            x = rows_v[pl.ds(yy * 4, 4)].reshape(rows_chunk, dim)
            r = jnp.dot(x, wgu_v[n], preferred_element_type=F32)
            g = r[:, :HD]
            u = r[:, HD:]
            h_v[:, pl.ds(pl.multiple_of(n * HD, HD), HD)] = (g / (1.0 + jnp.exp(-g)) * u).astype(BF)

        @pl.when(s < n_y - 1)
        def _():
            y2 = lax.rem(y + step_off(s + 1), n_y)
            for x2 in range(2):
                q = y2 * 2 + x2
                ag_copy(chip, q).wait_recv()
                fw_copy(q, core).start()

        @pl.when(s > 0)
        def _():
            finish(lax.rem(y + step_off(s - 1), n_y))

        @pl.loop(0, dim // blk)
        def _(j):
            cols = pl.ds(pl.multiple_of(j * blk, blk), blk)
            o = jnp.dot(h_v[...], wd_v[:, cols], preferred_element_type=F32)
            part_v[pl.ds(yy * 4, 4), :, cols] = o.astype(BF).reshape(4, slots, blk)

        for x2 in range(2):
            sb_copy(yy * 2 + x2, 1 - core).start()

    finish(lax.rem(y + step_off(n_y - 1), n_y))

    @pl.loop(1, n_chip)
    def _(d):
        ch_copy(chip, lax.rem(chip + d, n_chip)).wait_recv()

    @pl.loop(1, n_exp)
    def _(d):
        a_copy(lax.rem(e + d, n_exp), e).wait_send()

    @pl.loop(0, dim // blk)
    def _(j):
        cols = pl.ds(pl.multiple_of(j * blk, blk), blk)
        rsb_v[chip, :, cols] = part_v[c, :, cols]
        r = jnp.sum(rsb_v[:, :, cols].astype(F32), axis=0)
        pk_v[:, :, cols] = r.reshape(n_exp, cap, blk).astype(BF)

    def r_copy(te, src_e):
        return remote(pk_v.at[te], ret_v.at[src_e], r_ss.at[te], r_rs.at[src_e], c, te)

    @pl.loop(1, n_exp)
    def _(d):
        r_copy(lax.rem(e + d, n_exp), e).start()

    ret_v[e] = pk_v[e]

    wt = chosen * jnp.where(first, comb_ref[0:1, :], comb_ref[1:2, :])
    w_hi = wt.astype(BF)
    w_lo = (wt - w_hi.astype(F32)).astype(BF)

    @pl.loop(1, n_exp)
    def _(d):
        r_copy(e, lax.rem(e + d, n_exp)).wait_recv()

    @pl.loop(0, dim // blk)
    def _(j):
        cols = pl.ds(pl.multiple_of(j * blk, blk), blk)
        r = ret_v[:, :, cols].astype(F32).reshape(slots, blk).astype(BF)
        o = lax.dot_general(w_hi, r, TN, preferred_element_type=F32)
        o = o + lax.dot_general(w_lo, r, TN, preferred_element_type=F32)
        out_ref[:, cols] = (mixed_v[:, cols] + o).astype(BF)

    @pl.loop(c + 1, n_ctx)
    def _(j):
        for cp in kv_pair(j, c):
            cp.wait_send()

    @pl.loop(1, n_exp)
    def _(d):
        te = lax.rem(e + d, n_exp)

        @pl.loop(0, n_ps)
        def _(n):
            ps_copy(n, te, e).wait_send()

        r_copy(te, e).wait_send()

    @pl.loop(1, n_chip)
    def _(d):
        q = lax.rem(chip + d, n_chip)
        ag_copy(q, chip).wait_send()
        ch_copy(q, chip).wait_send()

    @pl.loop(0, n_chip)
    def _(q):
        fw_copy(q, core).wait_send()
        sb_copy(q, 1 - core).wait_send()


def body(
    stream, queries, attn_keys, attn_values, out_weight, norm_gain, expert_ids, combine, w_gate, w_up, w_down
):
    n_ctx = lax.axis_size("ctx")
    n_exp = lax.axis_size("exp")
    span, qw = queries.shape
    toks, dim = stream.shape
    hid = w_gate.shape[2]
    heads = qw // HD
    cap = toks // 2
    slots = n_exp * cap
    n_chip = n_ctx // 2
    nt = hid // HD
    n_ps = 4
    vm = pl.BlockSpec(memory_space=pltpu.VMEM)
    hbm = pl.BlockSpec(memory_space=pl.ANY)
    dma = pltpu.SemaphoreType.DMA
    scratch = [
        pltpu.VMEM((n_ctx, span, HD), BF),
        pltpu.VMEM((n_ctx, span, HD), BF),
        pltpu.VMEM((heads, span, HD), F32),
        pltpu.VMEM((heads, span, HD), F32),
        pltpu.VMEM((heads, span, HD), F32),
        pltpu.VMEM((span, qw), BF),
        pltpu.VMEM((qw, dim), BF),
        pltpu.VMEM((nt, dim, 2 * HD), BF),
        pltpu.VMEM((hid, dim), BF),
        pltpu.VMEM((n_ps, n_exp, toks, dim // n_ps), BF),
        pltpu.VMEM((n_ps, n_exp, toks, dim // n_ps), BF),
        pltpu.VMEM((toks, dim), F32),
        pltpu.VMEM((toks, dim), BF),
        pltpu.VMEM((n_exp, cap, dim), BF),
        pltpu.VMEM((n_exp, cap, dim), BF),
        pltpu.VMEM((n_ctx, slots, dim), BF),
        pltpu.VMEM((4 * slots, hid), BF),
        pltpu.VMEM((n_ctx, slots, dim), BF),
        pltpu.VMEM((n_chip, slots, dim), BF),
        pltpu.VMEM((n_chip, slots, dim), BF),
        pltpu.VMEM((n_exp, cap, dim), BF),
        dma((3, nt)),
        dma((2, n_ctx)),
        dma((2, n_ctx)),
        dma((n_ps, n_exp)),
        dma((n_ps, n_exp)),
        dma((n_exp,)),
        dma((n_exp,)),
        dma((n_chip,)),
        dma((n_chip,)),
        dma((n_chip,)),
        dma((n_chip,)),
        dma((n_chip,)),
        dma((n_chip,)),
        dma((n_chip,)),
        dma((n_chip,)),
        dma((n_exp,)),
        dma((n_exp,)),
    ]
    return pl.pallas_call(
        functools.partial(layer_kernel, n_ctx, n_exp),
        out_shape=jax.ShapeDtypeStruct((toks, dim), BF),
        in_specs=[vm] * 7 + [hbm] * 4,
        out_specs=vm,
        scratch_shapes=scratch,
        compiler_params=pltpu.CompilerParams(
            collective_id=0, has_side_effects=True, vmem_limit_bytes=67_000_000
        ),
        name="decoder_layer",
    )(
        queries,
        attn_keys,
        attn_values,
        stream,
        norm_gain.reshape(1, dim),
        expert_ids.T,
        combine.T,
        out_weight,
        w_gate[0],
        w_up[0],
        w_down[0],
    )


def solution(mesh):
    in_specs = (
        P(("ctx", "exp"), None),
        P("ctx", "exp"),
        P("ctx", "exp"),
        P("ctx", "exp"),
        P("exp", None),
        P(),
        P(("ctx", "exp"), None),
        P(("ctx", "exp"), None),
        P("exp", None, "ctx"),
        P("exp", None, "ctx"),
        P("exp", "ctx", None),
    )
    out_specs = P(("ctx", "exp"), None)
    return jax.shard_map(body, mesh=mesh, in_specs=in_specs, out_specs=out_specs, check_vma=False)
```

```python
import functools
import math

import jax
import jax.numpy as jnp
from jax import lax
from jax.experimental import pallas as pl
from jax.experimental.pallas import tpu as pltpu
from jax.sharding import PartitionSpec as P

HD = 128
MESH = pl.DeviceIdType.MESH
NEG = -1e30
F32 = jnp.float32
BF = jnp.bfloat16
NT = (((1,), (1,)), ((), ()))
TN = (((0,), (0,)), ((), ()))


def layer_kernel(
    n_ctx,
    n_exp,
    q_ref,
    k_ref,
    v_ref,
    stream_ref,
    gain_ref,
    ids_ref,
    comb_ref,
    ow_hbm,
    wg_hbm,
    wu_hbm,
    wd_hbm,
    out_ref,
    k_all,
    v_all,
    m_s,
    l_s,
    acc_s,
    att_s,
    ow_v,
    wgu_v,
    wd_v,
    ps_v,
    pr_v,
    mixed_v,
    normed_v,
    pk_v,
    a2_v,
    rows_v,
    h_v,
    part_v,
    sib_v,
    rh0_v,
    rx1_v,
    rh1_v,
    rx0_v,
    ret_v,
    w_sem,
    kv_ss,
    kv_rs,
    kf_ss,
    ps_ss,
    ps_rs,
    a_ss,
    a_rs,
    ag_ss,
    ag_rs,
    rl_ss,
    fw_ss,
    fw_rs,
    sb_ss,
    sb_rs,
    c0_ss,
    c0_rs,
    x1_ss,
    x1_rs,
    c1_ss,
    c1_rs,
    x0_ss,
    x0_rs,
    r_ss,
    r_rs,
):
    c = lax.axis_index("ctx")
    e = lax.axis_index("exp")
    span = q_ref.shape[0]
    heads = q_ref.shape[1] // HD
    toks, dim = stream_ref.shape
    cap = pk_v.shape[1]
    slots = n_exp * cap
    n_chip = n_ctx // 2
    core = lax.rem(c, 2)
    chip = c // 2
    y = c // 4
    xh = lax.rem(chip, 2)
    partner = chip + 1 - 2 * xh
    sibling = chip * 2 + 1 - core
    n_y = n_ctx // 4
    nt = wgu_v.shape[0]
    n_ps = ps_v.shape[0]
    ps_cols = ps_v.shape[3]
    blk = 512
    w0 = rh0_v.shape[3]
    w1 = dim - w0
    begin = (w1, 0)
    width = (w0, w1)

    def piece(h):
        return pl.ds(begin[h], width[h])

    def each_block(h, do):
        @pl.loop(0, width[h] // blk)
        def _(j):
            near = pl.multiple_of(j * blk, blk)
            do(pl.ds(pl.multiple_of(begin[h] + near, blk), blk), pl.ds(near, blk))

    def remote(src, dst, ss, rs, tc, te):
        return pltpu.make_async_remote_copy(
            src_ref=src, dst_ref=dst, send_sem=ss, recv_sem=rs, device_id=(tc, te), device_id_type=MESH
        )

    def weight_copies(n):
        cols = pl.ds(pl.multiple_of(n * HD, HD), HD)
        return (
            pltpu.make_async_copy(wg_hbm.at[:, cols], wgu_v.at[n, :, pl.ds(0, HD)], w_sem.at[0, n]),
            pltpu.make_async_copy(wu_hbm.at[:, cols], wgu_v.at[n, :, pl.ds(HD, HD)], w_sem.at[1, n]),
        )

    ow_copy = pltpu.make_async_copy(ow_hbm, ow_v, w_sem.at[2, 0])
    wd_copy = pltpu.make_async_copy(wd_hbm, wd_v, w_sem.at[2, 1])
    ow_copy.start()

    barrier = pltpu.get_barrier_semaphore()
    pl.semaphore_signal(barrier, inc=1, device_id=(sibling, e), device_id_type=MESH)

    @pl.loop(1, n_chip)
    def _(d):
        tc = lax.rem(chip + d, n_chip) * 2 + core
        pl.semaphore_signal(barrier, inc=1, device_id=(tc, e), device_id_type=MESH)

    @pl.loop(1, n_exp)
    def _(d):
        pl.semaphore_signal(barrier, inc=1, device_id=(c, lax.rem(e + d, n_exp)), device_id_type=MESH)

    pl.semaphore_wait(barrier, n_chip + n_exp - 1)

    def kv_pair(to_chip, block):
        return (
            remote(k_ref, k_all.at[block], kv_ss.at[0, to_chip], kv_rs.at[0, block], to_chip * 2 + core, e),
            remote(v_ref, v_all.at[block], kv_ss.at[1, to_chip], kv_rs.at[1, block], to_chip * 2 + core, e),
        )

    def kv_own():
        return (
            remote(k_ref, k_all.at[c], kf_ss.at[0, chip], kv_rs.at[0, c], sibling, e),
            remote(v_ref, v_all.at[c], kf_ss.at[1, chip], kv_rs.at[1, c], sibling, e),
        )

    def kv_forward(q):
        b = q * 2 + core
        return (
            remote(k_all.at[b], k_all.at[b], kf_ss.at[0, q], kv_rs.at[0, b], sibling, e),
            remote(v_all.at[b], v_all.at[b], kf_ss.at[1, q], kv_rs.at[1, b], sibling, e),
        )

    @pl.when(core == 0)
    def _():
        for cp in kv_own():
            cp.start()

    @pl.loop(chip + 1, n_chip)
    def _(q):
        for cp in kv_pair(q, c):
            cp.start()

    @pl.loop(0, nt)
    def _(n):
        for cp in weight_copies(n):
            cp.start()

    wd_copy.start()

    k_all[c] = k_ref[...]
    v_all[c] = v_ref[...]

    @pl.loop(c + 1, y * 4 + 4)
    def _(j):
        k_all[j] = jnp.zeros(k_ref.shape, BF)
        v_all[j] = jnp.zeros(v_ref.shape, BF)

    m_s[...] = jnp.full(m_s.shape, NEG, F32)
    l_s[...] = jnp.zeros(l_s.shape, F32)
    acc_s[...] = jnp.zeros(acc_s.shape, F32)
    scale = 1.0 / math.sqrt(HD)

    def step_off(s):
        return s ^ (s // 2)

    def forward_group(g):
        @pl.loop(g * 2, jnp.minimum(g * 2 + 2, chip))
        def _(q):
            for cp in kv_pair(chip, q * 2 + core):
                cp.wait_recv()
            for cp in kv_forward(q):
                cp.start()

    forward_group(y)

    @pl.loop(0, n_y)
    def _(s):
        g = y - step_off(s)
        g2 = y - step_off(s + 1)

        @pl.when((s < n_y - 1) & (g2 >= 0))
        def _():
            forward_group(g2)

        @pl.when(g >= 0)
        def _():
            @pl.loop(g * 2, jnp.minimum(g * 2 + 2, (c + core) // 2))
            def _(q):
                for cp in kv_pair(chip, q * 2 + 1 - core):
                    cp.wait_recv()

            keys = k_all[pl.ds(g * 4, 4)].reshape(4 * span, HD)
            vals = v_all[pl.ds(g * 4, 4)].reshape(4 * span, HD)
            row = lax.broadcasted_iota(jnp.int32, (span, 4 * span), 0) + (c - g * 4) * span
            col = lax.broadcasted_iota(jnp.int32, (span, 4 * span), 1)
            allowed = row >= col
            for h in range(heads):
                q_h = q_ref[:, h * HD : (h + 1) * HD]
                s_h = lax.dot_general(q_h, keys, NT, preferred_element_type=F32) * scale
                s_h = jnp.where(allowed, s_h, NEG)
                m_old = m_s[h]
                m_new = jnp.maximum(m_old, jnp.max(s_h, axis=1, keepdims=True))
                p = jnp.exp(s_h - m_new[:, :1])
                fix = jnp.exp(m_old - m_new)
                l_s[h] = l_s[h] * fix + jnp.sum(p, axis=1, keepdims=True)
                acc_s[h] = acc_s[h] * fix + jnp.dot(p.astype(BF), vals, preferred_element_type=F32)
                m_s[h] = m_new

    for h in range(heads):
        att_s[:, h * HD : (h + 1) * HD] = (acc_s[h] / l_s[h]).astype(BF)

    ow_copy.wait()

    def ps_copy(n, te, src_e):
        return remote(ps_v.at[n, te], pr_v.at[n, src_e], ps_ss.at[n, te], ps_rs.at[n, src_e], c, te)

    @pl.loop(0, n_ps)
    def _(n):
        cols = pl.ds(pl.multiple_of(n * ps_cols, ps_cols), ps_cols)
        r = jnp.dot(att_s[...], ow_v[:, cols], preferred_element_type=F32)
        ps_v[n] = r.reshape(n_exp, toks, ps_cols).astype(BF)

        @pl.loop(1, n_exp)
        def _(d):
            ps_copy(n, lax.rem(e + d, n_exp), e).start()

        pr_v[n, e] = ps_v[n, e]

    slot_row = lax.broadcasted_iota(jnp.int32, (slots, toks), 0)
    slot_exp = slot_row // cap
    first = ids_ref[0:1, :] == slot_exp
    second = ids_ref[1:2, :] == slot_exp
    named = jnp.where(first | second, 1.0, 0.0)
    tri = jnp.where(
        lax.broadcasted_iota(jnp.int32, (toks, toks), 0) < lax.broadcasted_iota(jnp.int32, (toks, toks), 1), 1.0, 0.0
    )
    rank = jnp.dot(named.astype(BF), tri.astype(BF), preferred_element_type=F32)
    slot_rank = (slot_row - slot_exp * cap).astype(F32)
    chosen = jnp.where(rank == slot_rank, named, 0.0)
    chosen_bf = chosen.astype(BF)

    @pl.loop(0, n_ps)
    def _(n):
        @pl.loop(1, n_exp)
        def _(d):
            ps_copy(n, e, lax.rem(e + d, n_exp)).wait_recv()

        cols = pl.ds(pl.multiple_of(n * ps_cols, ps_cols), ps_cols)
        total = jnp.sum(pr_v[n].astype(F32), axis=0)
        mixed_v[:, cols] = stream_ref[:, cols].astype(F32) + total

    mixed = mixed_v[...]
    mean_sq = jnp.mean(mixed * mixed, axis=1, keepdims=True)
    normed_v[...] = (mixed * lax.rsqrt(mean_sq + 1e-05) * gain_ref[...]).astype(BF)

    def a_copy(te, src_e, h):
        return remote(
            pk_v.at[te, :, piece(h)], a2_v.at[src_e, :, piece(h)], a_ss.at[h, te], a_rs.at[h, src_e], c, te
        )

    for h in (0, 1):

        def pick(cols, near):
            r = jnp.dot(chosen_bf, normed_v[:, cols], preferred_element_type=F32)
            pk_v[:, :, cols] = r.reshape(n_exp, cap, blk).astype(BF)

        each_block(h, pick)

        @pl.loop(1, n_exp)
        def _(d):
            a_copy(lax.rem(e + d, n_exp), e, h).start()

    a2_v[e] = pk_v[e]

    def row_copy(to_chip, q, h, ss):
        part = rows_v.at[q * 2 + core, :, piece(h)]
        return remote(part, part, ss, ag_rs.at[h, q], to_chip * 2 + core, e)

    def own_copy(to_chip, h):
        return row_copy(to_chip, chip, h, ag_ss.at[h, to_chip])

    def arrived(q, h):
        row_copy(chip, q, h, ag_ss.at[h, chip]).wait_recv()

    def relay_y(ty):
        return row_copy(ty * 2 + xh, partner, 0, rl_ss.at[0, ty])

    def relay_x(yy):
        return row_copy(partner, yy * 2 + xh, 1, rl_ss.at[1, yy])

    def fw_copy(q, of_core, h):
        part = rows_v.at[q * 2 + of_core, :, piece(h)]
        return remote(part, part, fw_ss.at[h, q], fw_rs.at[h, q], sibling, e)

    def down_y(s):
        return lax.rem(y + n_y - step_off(s), n_y)

    def up_y(s):
        return lax.rem(y + step_off(s), n_y)

    for h in (0, 1):

        @pl.loop(1, n_exp)
        def _(d):
            a_copy(e, lax.rem(e + d, n_exp), h).wait_recv()

        def settle(cols, near):
            rows_v[c, :, cols] = a2_v[:, :, cols].astype(F32).reshape(slots, blk).astype(BF)

        each_block(h, settle)
        own_copy(partner, h).start()

        @pl.loop(1, n_y)
        def _(s):
            own_copy(down_y(s) * 2 + xh, h).start()

        fw_copy(chip, core, h).start()

    def column_rows(s):
        q = up_y(s) * 2 + xh
        arrived(q, 0)
        fw_copy(q, core, 0).start()
        arrived(q, 1)
        relay_x(up_y(s)).start()
        fw_copy(q, core, 1).start()

    def other_rows(s):
        q = up_y(s) * 2 + 1 - xh
        for h in (0, 1):
            arrived(q, h)
            fw_copy(q, core, h).start()

    arrived(partner, 0)

    @pl.loop(1, n_y)
    def _(s):
        relay_y(down_y(s)).start()

    fw_copy(partner, core, 0).start()
    arrived(partner, 1)
    fw_copy(partner, core, 1).start()

    @pl.loop(1, n_y - 1)
    def _(s):
        column_rows(s)

    @pl.loop(0, nt)
    def _(n):
        for cp in weight_copies(n):
            cp.wait()

    wd_copy.wait()

    def sb_copy(q, of_core, h):
        return remote(
            part_v.at[q * 2 + of_core, :, piece(h)],
            sib_v.at[q, :, piece(h)],
            sb_ss.at[h, q],
            sb_rs.at[h, q],
            sibling,
            e,
        )

    def c0_copy(yy, x2, src_y):
        return remote(
            part_v.at[(yy * 2 + x2) * 2 + core, :, piece(0)],
            rh0_v.at[src_y, x2],
            c0_ss.at[yy, x2],
            c0_rs.at[src_y, x2],
            (yy * 2 + xh) * 2 + core,
            e,
        )

    def x1_copy(yy):
        return remote(
            part_v.at[(yy * 2 + 1 - xh) * 2 + core, :, piece(1)],
            rx1_v.at[yy],
            x1_ss.at[yy],
            x1_rs.at[yy],
            partner * 2 + core,
            e,
        )

    def c1_copy(yy, src_y):
        b = (yy * 2 + xh) * 2 + core
        return remote(part_v.at[b, :, piece(1)], rh1_v.at[src_y], c1_ss.at[yy], c1_rs.at[src_y], b, e)

    def x0_copy():
        return remote(
            part_v.at[partner * 2 + core, :, piece(0)], rx0_v, x0_ss.at[0], x0_rs.at[0], partner * 2 + core, e
        )

    def over_cores(yy):
        for h in (1, 0):
            for x2 in range(2):
                q = yy * 2 + x2
                b = q * 2 + core
                sb_copy(q, core, h).wait_recv()

                def add(cols, near):
                    total = part_v[b, :, cols].astype(F32) + sib_v[q, :, cols].astype(F32)
                    part_v[b, :, cols] = total.astype(BF)

                each_block(h, add)
            if h == 1:
                x1_copy(yy).start()
            else:

                @pl.when(yy != y)
                def _():
                    for x2 in range(2):
                        c0_copy(yy, x2, y).start()

    def over_x(yy):
        x1_copy(yy).wait_recv()
        b = (yy * 2 + xh) * 2 + core

        def add(cols, near):
            total = part_v[b, :, cols].astype(F32) + rx1_v[yy, :, near].astype(F32)
            part_v[b, :, cols] = total.astype(BF)

        each_block(1, add)

        @pl.when(yy != y)
        def _():
            c1_copy(yy, y).start()

    rows_chunk = 4 * slots
    dn = 1024

    @pl.loop(0, n_y)
    def _(s):
        yy = up_y(s)

        @pl.when(s == 1)
        def _():
            other_rows(1)

        for x2 in range(2):
            for h in (0, 1):
                fw_copy(yy * 2 + x2, 1 - core, h).wait_recv()

        @pl.loop(0, nt)
        def _(n):
            x = rows_v[pl.ds(yy * 4, 4)].reshape(rows_chunk, dim)
            r = jnp.dot(x, wgu_v[n], preferred_element_type=F32)
            g = r[:, :HD]
            u = r[:, HD:]
            h_v[:, pl.ds(pl.multiple_of(n * HD, HD), HD)] = (g / (1.0 + jnp.exp(-g)) * u).astype(BF)

        @pl.when(s == 0)
        def _():
            column_rows(n_y - 1)

        @pl.when((s > 0) & (s < n_y - 1))
        def _():
            other_rows(s + 1)

        @pl.when(s > 0)
        def _():
            over_cores(up_y(s - 1))

        @pl.when(s > 1)
        def _():
            over_x(up_y(s - 2))

        def down(j):
            cols = pl.ds(pl.multiple_of(j * dn, dn), dn)
            o = jnp.dot(h_v[...], wd_v[:, cols], preferred_element_type=F32)
            part_v[pl.ds(yy * 4, 4), :, cols] = o.astype(BF).reshape(4, slots, dn)

        early = -(-w1 // dn)
        pl.loop(0, early)(down)
        for x2 in range(2):
            sb_copy(yy * 2 + x2, 1 - core, 1).start()
        pl.loop(early, dim // dn)(down)
        for x2 in range(2):
            sb_copy(yy * 2 + x2, 1 - core, 0).start()

    over_cores(up_y(n_y - 1))
    over_x(up_y(n_y - 2))
    over_x(up_y(n_y - 1))

    @pl.loop(1, n_y)
    def _(d):
        for x2 in range(2):
            c0_copy(y, x2, lax.rem(y + d, n_y)).wait_recv()

    def column_sum(b, x2, cols, near):
        total = part_v[b, :, cols].astype(F32)
        for d in range(1, n_y):
            total = total + rh0_v[lax.rem(y + d, n_y), x2, :, near].astype(F32)
        return total

    def to_partner(cols, near):
        b = partner * 2 + core
        part_v[b, :, cols] = column_sum(b, 1 - xh, cols, near).astype(BF)

    each_block(0, to_partner)
    x0_copy().start()

    def r_copy(te, src_e, h):
        return remote(
            pk_v.at[te, :, piece(h)], ret_v.at[src_e, :, piece(h)], r_ss.at[h, te], r_rs.at[h, src_e], c, te
        )

    @pl.loop(1, n_exp)
    def _(d):
        for h in (0, 1):
            a_copy(lax.rem(e + d, n_exp), e, h).wait_send()

    def give_back(cols, total):
        pk_v[:, :, cols] = total.reshape(n_exp, cap, blk).astype(BF)

    for h in (1, 0):
        if h == 1:

            @pl.loop(1, n_y)
            def _(d):
                c1_copy(y, lax.rem(y + d, n_y)).wait_recv()

            def whole(cols, near):
                total = part_v[c, :, cols].astype(F32)
                for d in range(1, n_y):
                    total = total + rh1_v[lax.rem(y + d, n_y), :, near].astype(F32)
                give_back(cols, total)

        else:
            x0_copy().wait_recv()

            def whole(cols, near):
                give_back(cols, column_sum(c, xh, cols, near) + rx0_v[:, near].astype(F32))

        each_block(h, whole)

        @pl.loop(1, n_exp)
        def _(d):
            r_copy(lax.rem(e + d, n_exp), e, h).start()

    ret_v[e] = pk_v[e]

    wt = chosen * jnp.where(first, comb_ref[0:1, :], comb_ref[1:2, :])
    w_hi = wt.astype(BF)
    w_lo = (wt - w_hi.astype(F32)).astype(BF)

    for h in (1, 0):

        @pl.loop(1, n_exp)
        def _(d):
            r_copy(e, lax.rem(e + d, n_exp), h).wait_recv()

        def combine(cols, near):
            r = ret_v[:, :, cols].astype(F32).reshape(slots, blk).astype(BF)
            o = lax.dot_general(w_hi, r, TN, preferred_element_type=F32)
            o = o + lax.dot_general(w_lo, r, TN, preferred_element_type=F32)
            out_ref[:, cols] = (mixed_v[:, cols] + o).astype(BF)

        each_block(h, combine)

    @pl.when(core == 0)
    def _():
        for cp in kv_own():
            cp.wait_send()

    @pl.loop(chip + 1, n_chip)
    def _(q):
        for cp in kv_pair(q, c):
            cp.wait_send()

    @pl.loop(0, chip)
    def _(q):
        for cp in kv_forward(q):
            cp.wait_send()

    @pl.loop(1, n_exp)
    def _(d):
        te = lax.rem(e + d, n_exp)

        @pl.loop(0, n_ps)
        def _(n):
            ps_copy(n, te, e).wait_send()

        for h in (0, 1):
            r_copy(te, e, h).wait_send()

    for h in (0, 1):
        own_copy(partner, h).wait_send()

        @pl.loop(0, n_chip)
        def _(q):
            fw_copy(q, core, h).wait_send()
            sb_copy(q, 1 - core, h).wait_send()

    @pl.loop(1, n_y)
    def _(s):
        yy = up_y(s)
        for h in (0, 1):
            own_copy(yy * 2 + xh, h).wait_send()
        relay_y(yy).wait_send()
        relay_x(yy).wait_send()
        for x2 in range(2):
            c0_copy(yy, x2, y).wait_send()
        c1_copy(yy, y).wait_send()

    @pl.loop(0, n_y)
    def _(yy):
        x1_copy(yy).wait_send()

    x0_copy().wait_send()


def body(
    stream, queries, attn_keys, attn_values, out_weight, norm_gain, expert_ids, combine, w_gate, w_up, w_down
):
    n_ctx = lax.axis_size("ctx")
    n_exp = lax.axis_size("exp")
    span, qw = queries.shape
    toks, dim = stream.shape
    hid = w_gate.shape[2]
    heads = qw // HD
    cap = toks // 2
    slots = n_exp * cap
    n_chip = n_ctx // 2
    nt = hid // HD
    n_ps = 4
    n_y = n_ctx // 4
    w0 = dim * 3 // 8
    vm = pl.BlockSpec(memory_space=pltpu.VMEM)
    hbm = pl.BlockSpec(memory_space=pl.ANY)
    dma = pltpu.SemaphoreType.DMA
    scratch = [
        pltpu.VMEM((n_ctx, span, HD), BF),
        pltpu.VMEM((n_ctx, span, HD), BF),
        pltpu.VMEM((heads, span, HD), F32),
        pltpu.VMEM((heads, span, HD), F32),
        pltpu.VMEM((heads, span, HD), F32),
        pltpu.VMEM((span, qw), BF),
        pltpu.VMEM((qw, dim), BF),
        pltpu.VMEM((nt, dim, 2 * HD), BF),
        pltpu.VMEM((hid, dim), BF),
        pltpu.VMEM((n_ps, n_exp, toks, dim // n_ps), BF),
        pltpu.VMEM((n_ps, n_exp, toks, dim // n_ps), BF),
        pltpu.VMEM((toks, dim), F32),
        pltpu.VMEM((toks, dim), BF),
        pltpu.VMEM((n_exp, cap, dim), BF),
        pltpu.VMEM((n_exp, cap, dim), BF),
        pltpu.VMEM((n_ctx, slots, dim), BF),
        pltpu.VMEM((4 * slots, hid), BF),
        pltpu.VMEM((n_ctx, slots, dim), BF),
        pltpu.VMEM((n_chip, slots, dim), BF),
        pltpu.VMEM((n_y, 2, slots, w0), BF),
        pltpu.VMEM((n_y, slots, dim - w0), BF),
        pltpu.VMEM((n_y, slots, dim - w0), BF),
        pltpu.VMEM((slots, w0), BF),
        pltpu.VMEM((n_exp, cap, dim), BF),
        dma((3, nt)),
        dma((2, n_chip)),
        dma((2, n_ctx)),
        dma((2, n_chip)),
        dma((n_ps, n_exp)),
        dma((n_ps, n_exp)),
        dma((2, n_exp)),
        dma((2, n_exp)),
        dma((2, n_chip)),
        dma((2, n_chip)),
        dma((2, n_y)),
        dma((2, n_chip)),
        dma((2, n_chip)),
        dma((2, n_chip)),
        dma((2, n_chip)),
        dma((n_y, 2)),
        dma((n_y, 2)),
        dma((n_y,)),
        dma((n_y,)),
        dma((n_y,)),
        dma((n_y,)),
        dma((1,)),
        dma((1,)),
        dma((2, n_exp)),
        dma((2, n_exp)),
    ]
    return pl.pallas_call(
        functools.partial(layer_kernel, n_ctx, n_exp),
        out_shape=jax.ShapeDtypeStruct((toks, dim), BF),
        in_specs=[vm] * 7 + [hbm] * 4,
        out_specs=vm,
        scratch_shapes=scratch,
        compiler_params=pltpu.CompilerParams(
            collective_id=0, has_side_effects=True, vmem_limit_bytes=67_000_000
        ),
        name="decoder_layer",
    )(
        queries,
        attn_keys,
        attn_values,
        stream,
        norm_gain.reshape(1, dim),
        expert_ids.T,
        combine.T,
        out_weight,
        w_gate[0],
        w_up[0],
        w_down[0],
    )


def solution(mesh):
    in_specs = (
        P(("ctx", "exp"), None),
        P("ctx", "exp"),
        P("ctx", "exp"),
        P("ctx", "exp"),
        P("exp", None),
        P(),
        P(("ctx", "exp"), None),
        P(("ctx", "exp"), None),
        P("exp", None, "ctx"),
        P("exp", None, "ctx"),
        P("exp", "ctx", None),
    )
    out_specs = P(("ctx", "exp"), None)
    return jax.shard_map(body, mesh=mesh, in_specs=in_specs, out_specs=out_specs, check_vma=False)
```

```python
import functools
import math

import jax
import jax.numpy as jnp
from jax import lax
from jax.experimental import pallas as pl
from jax.experimental.pallas import tpu as pltpu
from jax.sharding import PartitionSpec as P

HD = 128
MESH = pl.DeviceIdType.MESH
NEG = -1e30
F32 = jnp.float32
BF = jnp.bfloat16
NT = (((1,), (1,)), ((), ()))
TN = (((0,), (0,)), ((), ()))


def layer_kernel(
    n_ctx,
    n_exp,
    q_ref,
    k_ref,
    v_ref,
    stream_ref,
    gain_ref,
    ids_ref,
    comb_ref,
    ow_hbm,
    wg_hbm,
    wu_hbm,
    wd_hbm,
    out_ref,
    k_all,
    v_all,
    m_s,
    l_s,
    acc_s,
    att_s,
    ow_v,
    wgu_v,
    wd_v,
    ps_v,
    pr_v,
    mixed_v,
    factor_v,
    pk_v,
    a2_v,
    rows_v,
    h_v,
    part_v,
    sib_v,
    rh0_v,
    rx1_v,
    rh1_v,
    rx0_v,
    ret_v,
    w_sem,
    kv_ss,
    kv_rs,
    kf_ss,
    ps_ss,
    ps_rs,
    a_ss,
    a_rs,
    ag_ss,
    ag_rs,
    rl_ss,
    fw_ss,
    fw_rs,
    sb_ss,
    sb_rs,
    c0_ss,
    c0_rs,
    x1_ss,
    x1_rs,
    c1_ss,
    c1_rs,
    x0_ss,
    x0_rs,
    r_ss,
    r_rs,
):
    c = lax.axis_index("ctx")
    e = lax.axis_index("exp")
    span = q_ref.shape[0]
    heads = q_ref.shape[1] // HD
    toks, dim = stream_ref.shape
    cap = pk_v.shape[1]
    slots = n_exp * cap
    n_chip = n_ctx // 2
    core = lax.rem(c, 2)
    chip = c // 2
    y = c // 4
    xh = lax.rem(chip, 2)
    partner = chip + 1 - 2 * xh
    sibling = chip * 2 + 1 - core
    n_y = n_ctx // 4
    nt = wgu_v.shape[0]
    n_ps = ps_v.shape[0]
    n_p = n_ps
    pw = dim // n_p
    w0 = rh0_v.shape[3] // n_p
    w1 = pw - w0
    g0 = pw * 3 // 8
    far = rows_v.shape[2] - dim

    def extra(p):
        return far if p == n_p - 1 else 0

    def whole_cols(p):
        return pl.ds(p * pw, pw)

    def sent_cols(p):
        return pl.ds(p * pw, pw + extra(p))

    def route_cols(p, h):
        return pl.ds(p * pw, w1) if h else pl.ds(p * pw + w1, w0)

    def sent_route_cols(p, h):
        return pl.ds(p * pw, pw - g0) if h else pl.ds(p * pw + pw - g0, g0 + extra(p))

    def near(p, h):
        return pl.ds(p * w1, w1) if h else pl.ds(p * w0, w0)

    def remote(src, dst, ss, rs, tc, te):
        return pltpu.make_async_remote_copy(
            src_ref=src, dst_ref=dst, send_sem=ss, recv_sem=rs, device_id=(tc, te), device_id_type=MESH
        )

    def weight_copies(n):
        cols = pl.ds(pl.multiple_of(n * HD, HD), HD)
        return (
            pltpu.make_async_copy(wg_hbm.at[:, cols], wgu_v.at[n, :, pl.ds(0, HD)], w_sem.at[0, n]),
            pltpu.make_async_copy(wu_hbm.at[:, cols], wgu_v.at[n, :, pl.ds(HD, HD)], w_sem.at[1, n]),
        )

    ow_copy = pltpu.make_async_copy(ow_hbm, ow_v, w_sem.at[2, 0])
    wd_copy = pltpu.make_async_copy(wd_hbm, wd_v, w_sem.at[2, 1])
    ow_copy.start()

    barrier = pltpu.get_barrier_semaphore()
    pl.semaphore_signal(barrier, inc=1, device_id=(sibling, e), device_id_type=MESH)

    @pl.loop(1, n_chip)
    def _(d):
        tc = lax.rem(chip + d, n_chip) * 2 + core
        pl.semaphore_signal(barrier, inc=1, device_id=(tc, e), device_id_type=MESH)

    @pl.loop(1, n_exp)
    def _(d):
        pl.semaphore_signal(barrier, inc=1, device_id=(c, lax.rem(e + d, n_exp)), device_id_type=MESH)

    pl.semaphore_wait(barrier, n_chip + n_exp - 1)

    def kv_pair(to_chip, block):
        return (
            remote(k_ref, k_all.at[block], kv_ss.at[0, to_chip], kv_rs.at[0, block], to_chip * 2 + core, e),
            remote(v_ref, v_all.at[block], kv_ss.at[1, to_chip], kv_rs.at[1, block], to_chip * 2 + core, e),
        )

    def kv_own():
        return (
            remote(k_ref, k_all.at[c], kf_ss.at[0, chip], kv_rs.at[0, c], sibling, e),
            remote(v_ref, v_all.at[c], kf_ss.at[1, chip], kv_rs.at[1, c], sibling, e),
        )

    def kv_forward(q):
        b = q * 2 + core
        return (
            remote(k_all.at[b], k_all.at[b], kf_ss.at[0, q], kv_rs.at[0, b], sibling, e),
            remote(v_all.at[b], v_all.at[b], kf_ss.at[1, q], kv_rs.at[1, b], sibling, e),
        )

    @pl.when(core == 0)
    def _():
        for cp in kv_own():
            cp.start()

    @pl.loop(chip + 1, n_chip)
    def _(q):
        for cp in kv_pair(q, c):
            cp.start()

    @pl.loop(0, nt)
    def _(n):
        for cp in weight_copies(n):
            cp.start()

    wd_copy.start()

    k_all[c] = k_ref[...]
    v_all[c] = v_ref[...]

    @pl.loop(c + 1, y * 4 + 4)
    def _(j):
        k_all[j] = jnp.zeros(k_ref.shape, BF)
        v_all[j] = jnp.zeros(v_ref.shape, BF)

    m_s[...] = jnp.full(m_s.shape, NEG, F32)
    l_s[...] = jnp.zeros(l_s.shape, F32)
    acc_s[...] = jnp.zeros(acc_s.shape, F32)
    scale = 1.0 / math.sqrt(HD)

    def step_off(s):
        return s ^ (s // 2)

    def forward_group(g):
        @pl.loop(g * 2, jnp.minimum(g * 2 + 2, chip))
        def _(q):
            for cp in kv_pair(chip, q * 2 + core):
                cp.wait_recv()
            for cp in kv_forward(q):
                cp.start()

    forward_group(y)

    @pl.loop(0, n_y)
    def _(s):
        g = y - step_off(s)
        g2 = y - step_off(s + 1)

        @pl.when((s < n_y - 1) & (g2 >= 0))
        def _():
            forward_group(g2)

        @pl.when(g >= 0)
        def _():
            @pl.loop(g * 2, jnp.minimum(g * 2 + 2, (c + core) // 2))
            def _(q):
                for cp in kv_pair(chip, q * 2 + 1 - core):
                    cp.wait_recv()

            keys = k_all[pl.ds(g * 4, 4)].reshape(4 * span, HD)
            vals = v_all[pl.ds(g * 4, 4)].reshape(4 * span, HD)
            row = lax.broadcasted_iota(jnp.int32, (span, 4 * span), 0) + (c - g * 4) * span
            col = lax.broadcasted_iota(jnp.int32, (span, 4 * span), 1)
            allowed = row >= col
            for h in range(heads):
                q_h = q_ref[:, h * HD : (h + 1) * HD]
                s_h = lax.dot_general(q_h, keys, NT, preferred_element_type=F32) * scale
                s_h = jnp.where(allowed, s_h, NEG)
                m_old = m_s[h]
                m_new = jnp.maximum(m_old, jnp.max(s_h, axis=1, keepdims=True))
                p = jnp.exp(s_h - m_new[:, :1])
                fix = jnp.exp(m_old - m_new)
                l_s[h] = l_s[h] * fix + jnp.sum(p, axis=1, keepdims=True)
                acc_s[h] = acc_s[h] * fix + jnp.dot(p.astype(BF), vals, preferred_element_type=F32)
                m_s[h] = m_new

    for h in range(heads):
        att_s[:, h * HD : (h + 1) * HD] = (acc_s[h] / l_s[h]).astype(BF)

    ow_copy.wait()

    def ps_copy(n, te, src_e):
        return remote(ps_v.at[n, te], pr_v.at[n, src_e], ps_ss.at[n, te], ps_rs.at[n, src_e], c, te)

    def project(n):
        r = jnp.dot(att_s[...], ow_v[:, whole_cols(n)], preferred_element_type=F32)
        ps_v[n] = r.reshape(n_exp, toks, pw).astype(BF)

        @pl.loop(1, n_exp)
        def _(d):
            ps_copy(n, lax.rem(e + d, n_exp), e).start()

        pr_v[n, e] = ps_v[n, e]

    project(0)
    project(1)

    slot_row = lax.broadcasted_iota(jnp.int32, (slots, toks), 0)
    slot_exp = slot_row // cap
    first = ids_ref[0:1, :] == slot_exp
    second = ids_ref[1:2, :] == slot_exp
    named = jnp.where(first | second, 1.0, 0.0)
    tri = jnp.where(
        lax.broadcasted_iota(jnp.int32, (toks, toks), 0) < lax.broadcasted_iota(jnp.int32, (toks, toks), 1), 1.0, 0.0
    )
    rank = jnp.dot(named.astype(BF), tri.astype(BF), preferred_element_type=F32)
    slot_rank = (slot_row - slot_exp * cap).astype(F32)
    chosen = jnp.where(rank == slot_rank, named, 0.0)
    chosen_bf = chosen.astype(BF)

    def a_copy(te, src_e, p):
        cols = sent_cols(p)
        return remote(pk_v.at[te, :, cols], a2_v.at[src_e, :, cols], a_ss.at[p, te], a_rs.at[p, src_e], c, te)

    def picked(values):
        r = jnp.dot(chosen_bf, values, preferred_element_type=F32)
        return r.reshape(n_exp, cap, values.shape[1]).astype(BF)

    def dispatch(p, square_sum):
        @pl.loop(1, n_exp)
        def _(d):
            ps_copy(p, e, lax.rem(e + d, n_exp)).wait_recv()

        cols = whole_cols(p)
        mixed = stream_ref[:, cols].astype(F32) + jnp.sum(pr_v[p].astype(F32), axis=0)
        mixed_v[:, cols] = mixed
        square_sum = square_sum + jnp.sum(mixed * mixed, axis=1, keepdims=True)
        pk_v[:, :, cols] = picked((mixed * gain_ref[:, cols]).astype(BF))
        if p == n_p - 1:
            factor = lax.rsqrt(square_sum / dim + 1e-05)
            high = factor.astype(BF).astype(F32)
            middle = (factor - high).astype(BF).astype(F32)
            low = factor - high - middle
            lane = lax.broadcasted_iota(jnp.int32, (toks, far), 1)
            terms = jnp.where(lane == 0, high, jnp.where(lane == 1, middle, jnp.where(lane == 2, low, 0.0)))
            pk_v[:, :, dim : dim + far] = picked(terms.astype(BF))

        @pl.loop(1, n_exp)
        def _(d):
            a_copy(lax.rem(e + d, n_exp), e, p).start()

        a2_v[e, :, sent_cols(p)] = pk_v[e, :, sent_cols(p)]
        return square_sum

    def row_copy(to_chip, q, p, cols, ss, rs):
        part = rows_v.at[q * 2 + core, :, cols]
        return remote(part, part, ss, rs, to_chip * 2 + core, e)

    def own_copy(to_chip, p):
        return row_copy(to_chip, chip, p, sent_cols(p), ag_ss.at[p, to_chip], ag_rs.at[0, p, chip])

    def arrived(q, p):
        row_copy(chip, q, p, sent_cols(p), ag_ss.at[p, chip], ag_rs.at[0, p, q]).wait_recv()

    def arrived_route(q, p, h):
        row_copy(chip, q, p, sent_route_cols(p, h), ag_ss.at[p, chip], ag_rs.at[h, p, q]).wait_recv()

    def relay_y(ty, p):
        return row_copy(ty * 2 + xh, partner, p, sent_route_cols(p, 0), rl_ss.at[0, p, ty], ag_rs.at[0, p, partner])

    def relay_x(yy, p):
        q = yy * 2 + xh
        return row_copy(partner, q, p, sent_route_cols(p, 1), rl_ss.at[1, p, yy], ag_rs.at[1, p, q])

    def fw_copy(q, of_core, p):
        part = rows_v.at[q * 2 + of_core, :, sent_cols(p)]
        return remote(part, part, fw_ss.at[p, q], fw_rs.at[p, q], sibling, e)

    def row_off(s):
        return lax.rem(s, 2) * 2 + s // 2

    def down_y(s):
        return lax.rem(y + n_y - row_off(s), n_y)

    def up_y(s):
        return lax.rem(y + row_off(s), n_y)

    def spread(p):
        @pl.loop(1, n_exp)
        def _(d):
            a_copy(e, lax.rem(e + d, n_exp), p).wait_recv()

        cols = sent_cols(p)
        rows_v[c, :, cols] = a2_v[:, :, cols].astype(F32).reshape(slots, pw + extra(p)).astype(BF)
        own_copy(partner, p).start()

        @pl.loop(1, n_y)
        def _(s):
            own_copy(down_y(s) * 2 + xh, p).start()

        fw_copy(chip, core, p).start()

    def partner_rows(p):
        arrived(partner, p)

        @pl.loop(1, n_y)
        def _(s):
            relay_y(down_y(s), p).start()

        fw_copy(partner, core, p).start()

    def column_rows(s, p):
        q = up_y(s) * 2 + xh
        arrived(q, p)
        relay_x(up_y(s), p).start()
        fw_copy(q, core, p).start()

    def near_rows(p):
        partner_rows(p)

        @pl.loop(1, n_y - 1)
        def _(s):
            column_rows(s, p)

    def other_rows(s, p):
        q = up_y(s) * 2 + 1 - xh
        for h in (0, 1):
            arrived_route(q, p, h)
        fw_copy(q, core, p).start()

    square_sum = jnp.zeros((toks, 1), F32)
    for p in range(n_p):
        square_sum = dispatch(p, square_sum)
        if p + 2 < n_p:
            project(p + 2)
        if p >= 1:
            spread(p - 1)
        if p >= 2:
            near_rows(p - 2)
    spread(n_p - 1)
    near_rows(n_p - 2)
    near_rows(n_p - 1)
    for p in range(n_p - 1):
        column_rows(n_y - 1, p)

    @pl.loop(0, nt)
    def _(n):
        for cp in weight_copies(n):
            cp.wait()

    wd_copy.wait()

    def sb_copy(q, of_core, p):
        cols = whole_cols(p)
        return remote(
            part_v.at[q * 2 + of_core, :, cols], sib_v.at[q, :, cols], sb_ss.at[p, q], sb_rs.at[p, q], sibling, e
        )

    def c0_copy(yy, x2, src_y, p):
        return remote(
            part_v.at[(yy * 2 + x2) * 2 + core, :, route_cols(p, 0)],
            rh0_v.at[src_y, x2, :, near(p, 0)],
            c0_ss.at[p, yy, x2],
            c0_rs.at[p, src_y, x2],
            (yy * 2 + xh) * 2 + core,
            e,
        )

    def x1_copy(yy, p):
        return remote(
            part_v.at[(yy * 2 + 1 - xh) * 2 + core, :, route_cols(p, 1)],
            rx1_v.at[yy, :, near(p, 1)],
            x1_ss.at[p, yy],
            x1_rs.at[p, yy],
            partner * 2 + core,
            e,
        )

    def c1_copy(yy, src_y, p):
        b = (yy * 2 + xh) * 2 + core
        return remote(
            part_v.at[b, :, route_cols(p, 1)],
            rh1_v.at[src_y, :, near(p, 1)],
            c1_ss.at[p, yy],
            c1_rs.at[p, src_y],
            b,
            e,
        )

    def x0_copy(p):
        b = partner * 2 + core
        return remote(
            part_v.at[b, :, route_cols(p, 0)], rx0_v.at[:, near(p, 0)], x0_ss.at[p], x0_rs.at[p], b, e
        )

    def over_cores(yy, p):
        cols = whole_cols(p)
        for x2 in range(2):
            q = yy * 2 + x2
            b = q * 2 + core
            sb_copy(q, core, p).wait_recv()
            part_v[b, :, cols] = (part_v[b, :, cols].astype(F32) + sib_v[q, :, cols].astype(F32)).astype(BF)
        x1_copy(yy, p).start()

        @pl.when(yy != y)
        def _():
            for x2 in range(2):
                c0_copy(yy, x2, y, p).start()

    def over_x(yy, p):
        x1_copy(yy, p).wait_recv()
        b = (yy * 2 + xh) * 2 + core
        cols = route_cols(p, 1)
        part_v[b, :, cols] = (part_v[b, :, cols].astype(F32) + rx1_v[yy, :, near(p, 1)].astype(F32)).astype(BF)

        @pl.when(yy != y)
        def _():
            c1_copy(yy, y, p).start()

    rows_chunk = 4 * slots

    @pl.loop(0, n_y)
    def _(s):
        yy = up_y(s)

        @pl.when(s == 1)
        def _():
            for p in range(n_p):
                other_rows(1, p)

        for x2 in range(2):
            for p in range(n_p):
                fw_copy(yy * 2 + x2, 1 - core, p).wait_recv()

        terms = rows_v[pl.ds(yy * 4, 4), :, dim : dim + far].reshape(rows_chunk, far).astype(F32)
        factor_v[...] = jnp.broadcast_to(jnp.sum(terms, axis=1, keepdims=True), (rows_chunk, HD))

        @pl.loop(0, nt)
        def _(n):
            x = rows_v[pl.ds(yy * 4, 4), :, 0:dim].reshape(rows_chunk, dim)
            r = jnp.dot(x, wgu_v[n], preferred_element_type=F32)
            g = r[:, :HD] * factor_v[...]
            u = r[:, HD:] * factor_v[...]
            h_v[:, pl.ds(pl.multiple_of(n * HD, HD), HD)] = (g / (1.0 + jnp.exp(-g)) * u).astype(BF)

        @pl.when(s == 0)
        def _():
            column_rows(n_y - 1, n_p - 1)

        @pl.when((s > 0) & (s < n_y - 1))
        def _():
            for p in range(n_p):
                other_rows(s + 1, p)

        @pl.when(s > 0)
        def _():
            for p in range(n_p):
                over_cores(up_y(s - 1), p)

        @pl.when(s > 1)
        def _():
            for p in range(n_p):
                over_x(up_y(s - 2), p)

        for p in range(n_p):
            o = jnp.dot(h_v[...], wd_v[:, whole_cols(p)], preferred_element_type=F32)
            part_v[pl.ds(yy * 4, 4), :, whole_cols(p)] = o.astype(BF).reshape(4, slots, pw)
            for x2 in range(2):
                sb_copy(yy * 2 + x2, 1 - core, p).start()

    for p in range(n_p):
        over_cores(up_y(n_y - 1), p)
    for p in range(n_p):
        over_x(up_y(n_y - 2), p)
    for p in range(n_p):
        over_x(up_y(n_y - 1), p)

    def column_sum(b, x2, p):
        total = part_v[b, :, route_cols(p, 0)].astype(F32)
        for d in range(1, n_y):
            total = total + rh0_v[lax.rem(y + d, n_y), x2, :, near(p, 0)].astype(F32)
        return total

    for p in range(n_p):

        @pl.loop(1, n_y)
        def _(d):
            for x2 in range(2):
                c0_copy(y, x2, lax.rem(y + d, n_y), p).wait_recv()

        b = partner * 2 + core
        part_v[b, :, route_cols(p, 0)] = column_sum(b, 1 - xh, p).astype(BF)
        x0_copy(p).start()

    def r_copy(te, src_e, p):
        cols = whole_cols(p)
        return remote(pk_v.at[te, :, cols], ret_v.at[src_e, :, cols], r_ss.at[p, te], r_rs.at[p, src_e], c, te)

    for p in range(n_p):

        @pl.loop(1, n_exp)
        def _(d):
            a_copy(lax.rem(e + d, n_exp), e, p).wait_send()

        @pl.loop(1, n_y)
        def _(d):
            c1_copy(y, lax.rem(y + d, n_y), p).wait_recv()

        total = part_v[c, :, route_cols(p, 1)].astype(F32)
        for d in range(1, n_y):
            total = total + rh1_v[lax.rem(y + d, n_y), :, near(p, 1)].astype(F32)
        pk_v[:, :, route_cols(p, 1)] = total.reshape(n_exp, cap, w1).astype(BF)
        x0_copy(p).wait_recv()
        total = column_sum(c, xh, p) + rx0_v[:, near(p, 0)].astype(F32)
        pk_v[:, :, route_cols(p, 0)] = total.reshape(n_exp, cap, w0).astype(BF)

        @pl.loop(1, n_exp)
        def _(d):
            r_copy(lax.rem(e + d, n_exp), e, p).start()

        ret_v[e, :, whole_cols(p)] = pk_v[e, :, whole_cols(p)]

    wt = chosen * jnp.where(first, comb_ref[0:1, :], comb_ref[1:2, :])
    w_hi = wt.astype(BF)
    w_lo = (wt - w_hi.astype(F32)).astype(BF)

    for p in range(n_p):

        @pl.loop(1, n_exp)
        def _(d):
            r_copy(e, lax.rem(e + d, n_exp), p).wait_recv()

        cols = whole_cols(p)
        r = ret_v[:, :, cols].astype(F32).reshape(slots, pw).astype(BF)
        o = lax.dot_general(w_hi, r, TN, preferred_element_type=F32)
        o = o + lax.dot_general(w_lo, r, TN, preferred_element_type=F32)
        out_ref[:, cols] = (mixed_v[:, cols] + o).astype(BF)

    @pl.when(core == 0)
    def _():
        for cp in kv_own():
            cp.wait_send()

    @pl.loop(chip + 1, n_chip)
    def _(q):
        for cp in kv_pair(q, c):
            cp.wait_send()

    @pl.loop(0, chip)
    def _(q):
        for cp in kv_forward(q):
            cp.wait_send()

    for p in range(n_p):

        @pl.loop(1, n_exp)
        def _(d):
            te = lax.rem(e + d, n_exp)
            ps_copy(p, te, e).wait_send()
            r_copy(te, e, p).wait_send()

        own_copy(partner, p).wait_send()
        x0_copy(p).wait_send()

        @pl.loop(0, n_chip)
        def _(q):
            fw_copy(q, core, p).wait_send()
            sb_copy(q, 1 - core, p).wait_send()

        @pl.loop(1, n_y)
        def _(s):
            yy = up_y(s)
            own_copy(yy * 2 + xh, p).wait_send()
            relay_y(yy, p).wait_send()
            relay_x(yy, p).wait_send()
            for x2 in range(2):
                c0_copy(yy, x2, y, p).wait_send()
            c1_copy(yy, y, p).wait_send()

        @pl.loop(0, n_y)
        def _(yy):
            x1_copy(yy, p).wait_send()


def body(
    stream, queries, attn_keys, attn_values, out_weight, norm_gain, expert_ids, combine, w_gate, w_up, w_down
):
    n_ctx = lax.axis_size("ctx")
    n_exp = lax.axis_size("exp")
    span, qw = queries.shape
    toks, dim = stream.shape
    hid = w_gate.shape[2]
    heads = qw // HD
    cap = toks // 2
    slots = n_exp * cap
    n_chip = n_ctx // 2
    nt = hid // HD
    n_ps = 4
    n_y = n_ctx // 4
    w0 = dim * 3 // 8
    vm = pl.BlockSpec(memory_space=pltpu.VMEM)
    hbm = pl.BlockSpec(memory_space=pl.ANY)
    dma = pltpu.SemaphoreType.DMA
    scratch = [
        pltpu.VMEM((n_ctx, span, HD), BF),
        pltpu.VMEM((n_ctx, span, HD), BF),
        pltpu.VMEM((heads, span, HD), F32),
        pltpu.VMEM((heads, span, HD), F32),
        pltpu.VMEM((heads, span, HD), F32),
        pltpu.VMEM((span, qw), BF),
        pltpu.VMEM((qw, dim), BF),
        pltpu.VMEM((nt, dim, 2 * HD), BF),
        pltpu.VMEM((hid, dim), BF),
        pltpu.VMEM((n_ps, n_exp, toks, dim // n_ps), BF),
        pltpu.VMEM((n_ps, n_exp, toks, dim // n_ps), BF),
        pltpu.VMEM((toks, dim), F32),
        pltpu.VMEM((4 * slots, HD), F32),
        pltpu.VMEM((n_exp, cap, dim + HD), BF),
        pltpu.VMEM((n_exp, cap, dim + HD), BF),
        pltpu.VMEM((n_ctx, slots, dim + HD), BF),
        pltpu.VMEM((4 * slots, hid), BF),
        pltpu.VMEM((n_ctx, slots, dim), BF),
        pltpu.VMEM((n_chip, slots, dim), BF),
        pltpu.VMEM((n_y, 2, slots, w0), BF),
        pltpu.VMEM((n_y, slots, dim - w0), BF),
        pltpu.VMEM((n_y, slots, dim - w0), BF),
        pltpu.VMEM((slots, w0), BF),
        pltpu.VMEM((n_exp, cap, dim), BF),
        dma((3, nt)),
        dma((2, n_chip)),
        dma((2, n_ctx)),
        dma((2, n_chip)),
        dma((n_ps, n_exp)),
        dma((n_ps, n_exp)),
        dma((n_ps, n_exp)),
        dma((n_ps, n_exp)),
        dma((n_ps, n_chip)),
        dma((2, n_ps, n_chip)),
        dma((2, n_ps, n_y)),
        dma((n_ps, n_chip)),
        dma((n_ps, n_chip)),
        dma((n_ps, n_chip)),
        dma((n_ps, n_chip)),
        dma((n_ps, n_y, 2)),
        dma((n_ps, n_y, 2)),
        dma((n_ps, n_y)),
        dma((n_ps, n_y)),
        dma((n_ps, n_y)),
        dma((n_ps, n_y)),
        dma((n_ps,)),
        dma((n_ps,)),
        dma((n_ps, n_exp)),
        dma((n_ps, n_exp)),
    ]
    return pl.pallas_call(
        functools.partial(layer_kernel, n_ctx, n_exp),
        out_shape=jax.ShapeDtypeStruct((toks, dim), BF),
        in_specs=[vm] * 7 + [hbm] * 4,
        out_specs=vm,
        scratch_shapes=scratch,
        compiler_params=pltpu.CompilerParams(
            collective_id=0, has_side_effects=True, vmem_limit_bytes=67_000_000
        ),
        name="decoder_layer",
    )(
        queries,
        attn_keys,
        attn_values,
        stream,
        norm_gain.reshape(1, dim),
        expert_ids.T,
        combine.T,
        out_weight,
        w_gate[0],
        w_up[0],
        w_down[0],
    )


def solution(mesh):
    in_specs = (
        P(("ctx", "exp"), None),
        P("ctx", "exp"),
        P("ctx", "exp"),
        P("ctx", "exp"),
        P("exp", None),
        P(),
        P(("ctx", "exp"), None),
        P(("ctx", "exp"), None),
        P("exp", None, "ctx"),
        P("exp", None, "ctx"),
        P("exp", "ctx", None),
    )
    out_specs = P(("ctx", "exp"), None)
    return jax.shard_map(body, mesh=mesh, in_specs=in_specs, out_specs=out_specs, check_vma=False)
```

```python
import functools
import math

import jax
import jax.numpy as jnp
from jax import lax
from jax.experimental import pallas as pl
from jax.experimental.pallas import tpu as pltpu
from jax.sharding import PartitionSpec as P

HD = 128
MESH = pl.DeviceIdType.MESH
NEG = -1e30
F32 = jnp.float32
BF = jnp.bfloat16
NT = (((1,), (1,)), ((), ()))
TN = (((0,), (0,)), ((), ()))


def layer_kernel(
    n_ctx,
    n_exp,
    q_ref,
    k_ref,
    v_ref,
    stream_ref,
    gain_ref,
    ids_ref,
    comb_ref,
    ow_hbm,
    wg_hbm,
    wu_hbm,
    wd_hbm,
    out_ref,
    k_all,
    v_all,
    m_s,
    l_s,
    acc_s,
    att_s,
    ow_v,
    wgu_v,
    wd_v,
    ps_v,
    pr_v,
    mixed_v,
    factor_v,
    pk_v,
    a2_v,
    rows_v,
    h_v,
    part_v,
    sib_v,
    rh0_v,
    rx1_v,
    rh1_v,
    rx0_v,
    ret_v,
    w_sem,
    kv_ss,
    kv_rs,
    kf_ss,
    ps_ss,
    ps_rs,
    a_ss,
    a_rs,
    ag_ss,
    ag_rs,
    rl_ss,
    fw_ss,
    fw_rs,
    sb_ss,
    sb_rs,
    c0_ss,
    c0_rs,
    x1_ss,
    x1_rs,
    c1_ss,
    c1_rs,
    x0_ss,
    x0_rs,
    r_ss,
    r_rs,
):
    c = lax.axis_index("ctx")
    e = lax.axis_index("exp")
    span = q_ref.shape[0]
    heads = q_ref.shape[1] // HD
    toks, dim = stream_ref.shape
    cap = pk_v.shape[1]
    slots = n_exp * cap
    n_chip = n_ctx // 2
    core = lax.rem(c, 2)
    chip = c // 2
    y = c // 4
    xh = lax.rem(chip, 2)
    partner = chip + 1 - 2 * xh
    sibling = chip * 2 + 1 - core
    n_y = n_ctx // 4
    nt = wgu_v.shape[0]
    n_ps = ps_v.shape[0]
    n_p = n_ps
    pw = dim // n_p
    w0 = rh0_v.shape[3] // n_p
    w1 = pw - w0
    g0 = pw * 3 // 8
    far = rows_v.shape[2] - dim

    def extra(p):
        return far if p == n_p - 1 else 0

    def whole_cols(p):
        return pl.ds(p * pw, pw)

    def sent_cols(p):
        return pl.ds(p * pw, pw + extra(p))

    def route_cols(p, h):
        return pl.ds(p * pw, w1) if h else pl.ds(p * pw + w1, w0)

    def sent_route_cols(p, h):
        return pl.ds(p * pw, pw - g0) if h else pl.ds(p * pw + pw - g0, g0 + extra(p))

    def near(p, h):
        return pl.ds(p * w1, w1) if h else pl.ds(p * w0, w0)

    def remote(src, dst, ss, rs, tc, te):
        return pltpu.make_async_remote_copy(
            src_ref=src, dst_ref=dst, send_sem=ss, recv_sem=rs, device_id=(tc, te), device_id_type=MESH
        )

    def weight_copies(n):
        cols = pl.ds(pl.multiple_of(n * HD, HD), HD)
        return (
            pltpu.make_async_copy(wg_hbm.at[:, cols], wgu_v.at[n, :, pl.ds(0, HD)], w_sem.at[0, n]),
            pltpu.make_async_copy(wu_hbm.at[:, cols], wgu_v.at[n, :, pl.ds(HD, HD)], w_sem.at[1, n]),
        )

    ow_copy = pltpu.make_async_copy(ow_hbm, ow_v, w_sem.at[2, 0])
    wd_copy = pltpu.make_async_copy(wd_hbm, wd_v, w_sem.at[2, 1])
    ow_copy.start()

    barrier = pltpu.get_barrier_semaphore()
    pl.semaphore_signal(barrier, inc=1, device_id=(sibling, e), device_id_type=MESH)

    @pl.loop(1, n_chip)
    def _(d):
        tc = lax.rem(chip + d, n_chip) * 2 + core
        pl.semaphore_signal(barrier, inc=1, device_id=(tc, e), device_id_type=MESH)

    @pl.loop(1, n_exp)
    def _(d):
        pl.semaphore_signal(barrier, inc=1, device_id=(c, lax.rem(e + d, n_exp)), device_id_type=MESH)

    pl.semaphore_wait(barrier, n_chip + n_exp - 1)

    def kv_pair(to_chip, block):
        return (
            remote(k_ref, k_all.at[block], kv_ss.at[0, to_chip], kv_rs.at[0, block], to_chip * 2 + core, e),
            remote(v_ref, v_all.at[block], kv_ss.at[1, to_chip], kv_rs.at[1, block], to_chip * 2 + core, e),
        )

    def kv_own():
        return (
            remote(k_ref, k_all.at[c], kf_ss.at[0, chip], kv_rs.at[0, c], sibling, e),
            remote(v_ref, v_all.at[c], kf_ss.at[1, chip], kv_rs.at[1, c], sibling, e),
        )

    def kv_forward(q):
        b = q * 2 + core
        return (
            remote(k_all.at[b], k_all.at[b], kf_ss.at[0, q], kv_rs.at[0, b], sibling, e),
            remote(v_all.at[b], v_all.at[b], kf_ss.at[1, q], kv_rs.at[1, b], sibling, e),
        )

    @pl.when(core == 0)
    def _():
        for cp in kv_own():
            cp.start()

    @pl.loop(chip + 1, n_chip)
    def _(q):
        for cp in kv_pair(q, c):
            cp.start()

    @pl.loop(0, nt)
    def _(n):
        for cp in weight_copies(n):
            cp.start()

    wd_copy.start()

    k_all[c] = k_ref[...]
    v_all[c] = v_ref[...]

    @pl.loop(c + 1, y * 4 + 4)
    def _(j):
        k_all[j] = jnp.zeros(k_ref.shape, BF)
        v_all[j] = jnp.zeros(v_ref.shape, BF)

    m_s[...] = jnp.full(m_s.shape, NEG, F32)
    l_s[...] = jnp.zeros(l_s.shape, F32)
    acc_s[...] = jnp.zeros(acc_s.shape, F32)
    scale = 1.0 / math.sqrt(HD)

    def step_off(s):
        return s ^ (s // 2)

    def forward_group(g):
        @pl.loop(g * 2, jnp.minimum(g * 2 + 2, chip))
        def _(q):
            for cp in kv_pair(chip, q * 2 + core):
                cp.wait_recv()
            for cp in kv_forward(q):
                cp.start()

    forward_group(y)

    @pl.loop(0, n_y)
    def _(s):
        g = y - step_off(s)
        g2 = y - step_off(s + 1)

        @pl.when((s < n_y - 1) & (g2 >= 0))
        def _():
            forward_group(g2)

        @pl.when(g >= 0)
        def _():
            @pl.loop(g * 2, jnp.minimum(g * 2 + 2, (c + core) // 2))
            def _(q):
                for cp in kv_pair(chip, q * 2 + 1 - core):
                    cp.wait_recv()

            keys = k_all[pl.ds(g * 4, 4)].reshape(4 * span, HD)
            vals = v_all[pl.ds(g * 4, 4)].reshape(4 * span, HD)
            row = lax.broadcasted_iota(jnp.int32, (span, 4 * span), 0) + (c - g * 4) * span
            col = lax.broadcasted_iota(jnp.int32, (span, 4 * span), 1)
            allowed = row >= col
            for h in range(heads):
                q_h = q_ref[:, h * HD : (h + 1) * HD]
                s_h = lax.dot_general(q_h, keys, NT, preferred_element_type=F32) * scale
                s_h = jnp.where(allowed, s_h, NEG)
                m_old = m_s[h]
                m_new = jnp.maximum(m_old, jnp.max(s_h, axis=1, keepdims=True))
                p = jnp.exp(s_h - m_new[:, :1])
                fix = jnp.exp(m_old - m_new)
                l_s[h] = l_s[h] * fix + jnp.sum(p, axis=1, keepdims=True)
                acc_s[h] = acc_s[h] * fix + jnp.dot(p.astype(BF), vals, preferred_element_type=F32)
                m_s[h] = m_new

    for h in range(heads):
        att_s[:, h * HD : (h + 1) * HD] = (acc_s[h] / l_s[h]).astype(BF)

    ow_copy.wait()

    def ps_copy(n, te, src_e):
        return remote(ps_v.at[n, te], pr_v.at[n, src_e], ps_ss.at[n, te], ps_rs.at[n, src_e], c, te)

    def project(n):
        r = jnp.dot(att_s[...], ow_v[:, whole_cols(n)], preferred_element_type=F32)
        ps_v[n] = r.reshape(n_exp, toks, pw).astype(BF)

        @pl.loop(1, n_exp)
        def _(d):
            ps_copy(n, lax.rem(e + d, n_exp), e).start()

        pr_v[n, e] = ps_v[n, e]

    project(0)
    project(1)

    slot_row = lax.broadcasted_iota(jnp.int32, (slots, toks), 0)
    slot_exp = slot_row // cap
    first = ids_ref[0:1, :] == slot_exp
    second = ids_ref[1:2, :] == slot_exp
    named = jnp.where(first | second, 1.0, 0.0)
    tri = jnp.where(
        lax.broadcasted_iota(jnp.int32, (toks, toks), 0) < lax.broadcasted_iota(jnp.int32, (toks, toks), 1), 1.0, 0.0
    )
    rank = jnp.dot(named.astype(BF), tri.astype(BF), preferred_element_type=F32)
    slot_rank = (slot_row - slot_exp * cap).astype(F32)
    chosen = jnp.where(rank == slot_rank, named, 0.0)
    chosen_bf = chosen.astype(BF)

    def a_copy(te, src_e, p):
        cols = sent_cols(p)
        return remote(pk_v.at[te, :, cols], a2_v.at[src_e, :, cols], a_ss.at[p, te], a_rs.at[p, src_e], c, te)

    def picked(values):
        r = jnp.dot(chosen_bf, values, preferred_element_type=F32)
        return r.reshape(n_exp, cap, values.shape[1]).astype(BF)

    def dispatch(p, square_sum):
        @pl.loop(1, n_exp)
        def _(d):
            ps_copy(p, e, lax.rem(e + d, n_exp)).wait_recv()

        cols = whole_cols(p)
        mixed = stream_ref[:, cols].astype(F32) + jnp.sum(pr_v[p].astype(F32), axis=0)
        mixed_v[:, cols] = mixed
        square_sum = square_sum + jnp.sum(mixed * mixed, axis=1, keepdims=True)
        pk_v[:, :, cols] = picked((mixed * gain_ref[:, cols]).astype(BF))
        if p == n_p - 1:
            factor = lax.rsqrt(square_sum / dim + 1e-05)
            high = factor.astype(BF).astype(F32)
            middle = (factor - high).astype(BF).astype(F32)
            low = factor - high - middle
            lane = lax.broadcasted_iota(jnp.int32, (toks, far), 1)
            terms = jnp.where(lane == 0, high, jnp.where(lane == 1, middle, jnp.where(lane == 2, low, 0.0)))
            pk_v[:, :, dim : dim + far] = picked(terms.astype(BF))

        @pl.loop(1, n_exp)
        def _(d):
            a_copy(lax.rem(e + d, n_exp), e, p).start()

        a2_v[e, :, sent_cols(p)] = pk_v[e, :, sent_cols(p)]
        return square_sum

    def row_copy(to_chip, q, p, cols, ss, rs):
        part = rows_v.at[q * 2 + core, :, cols]
        return remote(part, part, ss, rs, to_chip * 2 + core, e)

    def own_copy(to_chip, p):
        return row_copy(to_chip, chip, p, sent_cols(p), ag_ss.at[p, to_chip], ag_rs.at[0, p, chip])

    def arrived(q, p):
        row_copy(chip, q, p, sent_cols(p), ag_ss.at[p, chip], ag_rs.at[0, p, q]).wait_recv()

    def arrived_route(q, p, h):
        row_copy(chip, q, p, sent_route_cols(p, h), ag_ss.at[p, chip], ag_rs.at[h, p, q]).wait_recv()

    def relay_y(ty, p):
        return row_copy(ty * 2 + xh, partner, p, sent_route_cols(p, 0), rl_ss.at[0, p, ty], ag_rs.at[0, p, partner])

    def relay_x(yy, p):
        q = yy * 2 + xh
        return row_copy(partner, q, p, sent_route_cols(p, 1), rl_ss.at[1, p, yy], ag_rs.at[1, p, q])

    def fw_copy(q, of_core, p):
        part = rows_v.at[q * 2 + of_core, :, sent_cols(p)]
        return remote(part, part, fw_ss.at[p, q], fw_rs.at[p, q], sibling, e)

    def row_off(s):
        return lax.rem(s, 2) * 2 + s // 2

    def down_y(s):
        return lax.rem(y + n_y - row_off(s), n_y)

    def up_y(s):
        return lax.rem(y + row_off(s), n_y)

    def spread(p):
        @pl.loop(1, n_exp)
        def _(d):
            a_copy(e, lax.rem(e + d, n_exp), p).wait_recv()

        cols = sent_cols(p)
        rows_v[c, :, cols] = a2_v[:, :, cols].astype(F32).reshape(slots, pw + extra(p)).astype(BF)
        own_copy(partner, p).start()

        @pl.loop(1, n_y)
        def _(s):
            own_copy(down_y(s) * 2 + xh, p).start()

        fw_copy(chip, core, p).start()

    def partner_rows(p):
        arrived(partner, p)

        @pl.loop(1, n_y)
        def _(s):
            relay_y(down_y(s), p).start()

        fw_copy(partner, core, p).start()

    def column_rows(s, p):
        q = up_y(s) * 2 + xh
        arrived(q, p)
        relay_x(up_y(s), p).start()
        fw_copy(q, core, p).start()

    def near_rows(p):
        partner_rows(p)

        @pl.loop(1, n_y - 1)
        def _(s):
            column_rows(s, p)

    def other_rows(s, p):
        q = up_y(s) * 2 + 1 - xh
        for h in (0, 1):
            arrived_route(q, p, h)
        fw_copy(q, core, p).start()

    square_sum = jnp.zeros((toks, 1), F32)
    for p in range(n_p):
        square_sum = dispatch(p, square_sum)
        if p + 2 < n_p:
            project(p + 2)
        if p >= 1:
            spread(p - 1)
        if p >= 2:
            near_rows(p - 2)
    spread(n_p - 1)
    near_rows(n_p - 2)
    near_rows(n_p - 1)
    for p in range(n_p - 1):
        column_rows(n_y - 1, p)

    @pl.loop(0, nt)
    def _(n):
        for cp in weight_copies(n):
            cp.wait()

    wd_copy.wait()

    def sb_copy(q, of_core, p):
        cols = whole_cols(p)
        return remote(
            part_v.at[q * 2 + of_core, :, cols], sib_v.at[q, :, cols], sb_ss.at[p, q], sb_rs.at[p, q], sibling, e
        )

    def c0_copy(yy, x2, src_y, p):
        return remote(
            part_v.at[(yy * 2 + x2) * 2 + core, :, route_cols(p, 0)],
            rh0_v.at[src_y, x2, :, near(p, 0)],
            c0_ss.at[p, yy, x2],
            c0_rs.at[p, src_y, x2],
            (yy * 2 + xh) * 2 + core,
            e,
        )

    def x1_copy(yy, p):
        return remote(
            part_v.at[(yy * 2 + 1 - xh) * 2 + core, :, route_cols(p, 1)],
            rx1_v.at[yy, :, near(p, 1)],
            x1_ss.at[p, yy],
            x1_rs.at[p, yy],
            partner * 2 + core,
            e,
        )

    def c1_copy(yy, src_y, p):
        b = (yy * 2 + xh) * 2 + core
        return remote(
            part_v.at[b, :, route_cols(p, 1)],
            rh1_v.at[src_y, :, near(p, 1)],
            c1_ss.at[p, yy],
            c1_rs.at[p, src_y],
            b,
            e,
        )

    def x0_copy(p):
        b = partner * 2 + core
        return remote(
            part_v.at[b, :, route_cols(p, 0)], rx0_v.at[:, near(p, 0)], x0_ss.at[p], x0_rs.at[p], b, e
        )

    def over_cores(yy, p):
        cols = whole_cols(p)
        for x2 in range(2):
            q = yy * 2 + x2
            b = q * 2 + core
            sb_copy(q, core, p).wait_recv()
            part_v[b, :, cols] = (part_v[b, :, cols].astype(F32) + sib_v[q, :, cols].astype(F32)).astype(BF)
        x1_copy(yy, p).start()

        @pl.when(yy != y)
        def _():
            for x2 in range(2):
                c0_copy(yy, x2, y, p).start()

    def over_x(yy, p):
        x1_copy(yy, p).wait_recv()
        b = (yy * 2 + xh) * 2 + core
        cols = route_cols(p, 1)
        part_v[b, :, cols] = (part_v[b, :, cols].astype(F32) + rx1_v[yy, :, near(p, 1)].astype(F32)).astype(BF)

        @pl.when(yy != y)
        def _():
            c1_copy(yy, y, p).start()

    rows_chunk = 4 * slots

    @pl.loop(0, n_y)
    def _(s):
        yy = up_y(s)

        @pl.when(s > 0)
        def _():
            for p in range(n_p):
                over_cores(up_y(s - 1), p)

        @pl.when(s == 1)
        def _():
            for p in range(n_p):
                other_rows(1, p)

        for x2 in range(2):
            for p in range(n_p):
                fw_copy(yy * 2 + x2, 1 - core, p).wait_recv()

        terms = rows_v[pl.ds(yy * 4, 4), :, dim : dim + far].reshape(rows_chunk, far).astype(F32)
        factor_v[...] = jnp.broadcast_to(jnp.sum(terms, axis=1, keepdims=True), (rows_chunk, HD))

        @pl.loop(0, nt)
        def _(n):
            x = rows_v[pl.ds(yy * 4, 4), :, 0:dim].reshape(rows_chunk, dim)
            r = jnp.dot(x, wgu_v[n], preferred_element_type=F32)
            g = r[:, :HD] * factor_v[...]
            u = r[:, HD:] * factor_v[...]
            h_v[:, pl.ds(pl.multiple_of(n * HD, HD), HD)] = (g / (1.0 + jnp.exp(-g)) * u).astype(BF)

        @pl.when(s == 0)
        def _():
            column_rows(n_y - 1, n_p - 1)

        @pl.when((s > 0) & (s < n_y - 1))
        def _():
            for p in range(n_p):
                other_rows(s + 1, p)

        for p in range(n_p):
            o = jnp.dot(h_v[...], wd_v[:, whole_cols(p)], preferred_element_type=F32)
            part_v[pl.ds(yy * 4, 4), :, whole_cols(p)] = o.astype(BF).reshape(4, slots, pw)
            for x2 in range(2):
                sb_copy(yy * 2 + x2, 1 - core, p).start()

        @pl.when((s > 0) & (s < n_y - 1))
        def _():
            for p in range(n_p):
                over_x(up_y(s - 1), p)

    for p in range(n_p):
        over_cores(up_y(n_y - 1), p)
    for p in range(n_p):
        over_x(up_y(n_y - 2), p)
    for p in range(n_p):
        over_x(up_y(n_y - 1), p)

    def column_sum(b, x2, p):
        total = part_v[b, :, route_cols(p, 0)].astype(F32)
        for d in range(1, n_y):
            total = total + rh0_v[lax.rem(y + d, n_y), x2, :, near(p, 0)].astype(F32)
        return total

    for p in range(n_p):

        @pl.loop(1, n_y)
        def _(d):
            for x2 in range(2):
                c0_copy(y, x2, lax.rem(y + d, n_y), p).wait_recv()

        b = partner * 2 + core
        part_v[b, :, route_cols(p, 0)] = column_sum(b, 1 - xh, p).astype(BF)
        x0_copy(p).start()

    def r_copy(te, src_e, p):
        cols = whole_cols(p)
        return remote(pk_v.at[te, :, cols], ret_v.at[src_e, :, cols], r_ss.at[p, te], r_rs.at[p, src_e], c, te)

    for p in range(n_p):

        @pl.loop(1, n_exp)
        def _(d):
            a_copy(lax.rem(e + d, n_exp), e, p).wait_send()

        @pl.loop(1, n_y)
        def _(d):
            c1_copy(y, lax.rem(y + d, n_y), p).wait_recv()

        total = part_v[c, :, route_cols(p, 1)].astype(F32)
        for d in range(1, n_y):
            total = total + rh1_v[lax.rem(y + d, n_y), :, near(p, 1)].astype(F32)
        pk_v[:, :, route_cols(p, 1)] = total.reshape(n_exp, cap, w1).astype(BF)
        x0_copy(p).wait_recv()
        total = column_sum(c, xh, p) + rx0_v[:, near(p, 0)].astype(F32)
        pk_v[:, :, route_cols(p, 0)] = total.reshape(n_exp, cap, w0).astype(BF)

        @pl.loop(1, n_exp)
        def _(d):
            r_copy(lax.rem(e + d, n_exp), e, p).start()

        ret_v[e, :, whole_cols(p)] = pk_v[e, :, whole_cols(p)]

    wt = chosen * jnp.where(first, comb_ref[0:1, :], comb_ref[1:2, :])
    w_hi = wt.astype(BF)
    w_lo = (wt - w_hi.astype(F32)).astype(BF)

    for p in range(n_p):

        @pl.loop(1, n_exp)
        def _(d):
            r_copy(e, lax.rem(e + d, n_exp), p).wait_recv()

        cols = whole_cols(p)
        r = ret_v[:, :, cols].astype(F32).reshape(slots, pw).astype(BF)
        o = lax.dot_general(w_hi, r, TN, preferred_element_type=F32)
        o = o + lax.dot_general(w_lo, r, TN, preferred_element_type=F32)
        out_ref[:, cols] = (mixed_v[:, cols] + o).astype(BF)

    @pl.when(core == 0)
    def _():
        for cp in kv_own():
            cp.wait_send()

    @pl.loop(chip + 1, n_chip)
    def _(q):
        for cp in kv_pair(q, c):
            cp.wait_send()

    @pl.loop(0, chip)
    def _(q):
        for cp in kv_forward(q):
            cp.wait_send()

    for p in range(n_p):

        @pl.loop(1, n_exp)
        def _(d):
            te = lax.rem(e + d, n_exp)
            ps_copy(p, te, e).wait_send()
            r_copy(te, e, p).wait_send()

        own_copy(partner, p).wait_send()
        x0_copy(p).wait_send()

        @pl.loop(0, n_chip)
        def _(q):
            fw_copy(q, core, p).wait_send()
            sb_copy(q, 1 - core, p).wait_send()

        @pl.loop(1, n_y)
        def _(s):
            yy = up_y(s)
            own_copy(yy * 2 + xh, p).wait_send()
            relay_y(yy, p).wait_send()
            relay_x(yy, p).wait_send()
            for x2 in range(2):
                c0_copy(yy, x2, y, p).wait_send()
            c1_copy(yy, y, p).wait_send()

        @pl.loop(0, n_y)
        def _(yy):
            x1_copy(yy, p).wait_send()


def body(
    stream, queries, attn_keys, attn_values, out_weight, norm_gain, expert_ids, combine, w_gate, w_up, w_down
):
    n_ctx = lax.axis_size("ctx")
    n_exp = lax.axis_size("exp")
    span, qw = queries.shape
    toks, dim = stream.shape
    hid = w_gate.shape[2]
    heads = qw // HD
    cap = toks // 2
    slots = n_exp * cap
    n_chip = n_ctx // 2
    nt = hid // HD
    n_ps = 4
    n_y = n_ctx // 4
    w0 = dim * 3 // 8
    vm = pl.BlockSpec(memory_space=pltpu.VMEM)
    hbm = pl.BlockSpec(memory_space=pl.ANY)
    dma = pltpu.SemaphoreType.DMA
    scratch = [
        pltpu.VMEM((n_ctx, span, HD), BF),
        pltpu.VMEM((n_ctx, span, HD), BF),
        pltpu.VMEM((heads, span, HD), F32),
        pltpu.VMEM((heads, span, HD), F32),
        pltpu.VMEM((heads, span, HD), F32),
        pltpu.VMEM((span, qw), BF),
        pltpu.VMEM((qw, dim), BF),
        pltpu.VMEM((nt, dim, 2 * HD), BF),
        pltpu.VMEM((hid, dim), BF),
        pltpu.VMEM((n_ps, n_exp, toks, dim // n_ps), BF),
        pltpu.VMEM((n_ps, n_exp, toks, dim // n_ps), BF),
        pltpu.VMEM((toks, dim), F32),
        pltpu.VMEM((4 * slots, HD), F32),
        pltpu.VMEM((n_exp, cap, dim + HD), BF),
        pltpu.VMEM((n_exp, cap, dim + HD), BF),
        pltpu.VMEM((n_ctx, slots, dim + HD), BF),
        pltpu.VMEM((4 * slots, hid), BF),
        pltpu.VMEM((n_ctx, slots, dim), BF),
        pltpu.VMEM((n_chip, slots, dim), BF),
        pltpu.VMEM((n_y, 2, slots, w0), BF),
        pltpu.VMEM((n_y, slots, dim - w0), BF),
        pltpu.VMEM((n_y, slots, dim - w0), BF),
        pltpu.VMEM((slots, w0), BF),
        pltpu.VMEM((n_exp, cap, dim), BF),
        dma((3, nt)),
        dma((2, n_chip)),
        dma((2, n_ctx)),
        dma((2, n_chip)),
        dma((n_ps, n_exp)),
        dma((n_ps, n_exp)),
        dma((n_ps, n_exp)),
        dma((n_ps, n_exp)),
        dma((n_ps, n_chip)),
        dma((2, n_ps, n_chip)),
        dma((2, n_ps, n_y)),
        dma((n_ps, n_chip)),
        dma((n_ps, n_chip)),
        dma((n_ps, n_chip)),
        dma((n_ps, n_chip)),
        dma((n_ps, n_y, 2)),
        dma((n_ps, n_y, 2)),
        dma((n_ps, n_y)),
        dma((n_ps, n_y)),
        dma((n_ps, n_y)),
        dma((n_ps, n_y)),
        dma((n_ps,)),
        dma((n_ps,)),
        dma((n_ps, n_exp)),
        dma((n_ps, n_exp)),
    ]
    return pl.pallas_call(
        functools.partial(layer_kernel, n_ctx, n_exp),
        out_shape=jax.ShapeDtypeStruct((toks, dim), BF),
        in_specs=[vm] * 7 + [hbm] * 4,
        out_specs=vm,
        scratch_shapes=scratch,
        compiler_params=pltpu.CompilerParams(
            collective_id=0, has_side_effects=True, vmem_limit_bytes=67_000_000
        ),
        name="decoder_layer",
    )(
        queries,
        attn_keys,
        attn_values,
        stream,
        norm_gain.reshape(1, dim),
        expert_ids.T,
        combine.T,
        out_weight,
        w_gate[0],
        w_up[0],
        w_down[0],
    )


def solution(mesh):
    in_specs = (
        P(("ctx", "exp"), None),
        P("ctx", "exp"),
        P("ctx", "exp"),
        P("ctx", "exp"),
        P("exp", None),
        P(),
        P(("ctx", "exp"), None),
        P(("ctx", "exp"), None),
        P("exp", None, "ctx"),
        P("exp", None, "ctx"),
        P("exp", "ctx", None),
    )
    out_specs = P(("ctx", "exp"), None)
    return jax.shard_map(body, mesh=mesh, in_specs=in_specs, out_specs=out_specs, check_vma=False)
```

```python
import functools
import math

import jax
import jax.numpy as jnp
from jax import lax
from jax.experimental import pallas as pl
from jax.experimental.pallas import tpu as pltpu
from jax.sharding import PartitionSpec as P

HD = 128
MESH = pl.DeviceIdType.MESH
NEG = -1e30
F32 = jnp.float32
BF = jnp.bfloat16
NT = (((1,), (1,)), ((), ()))
TN = (((0,), (0,)), ((), ()))


def layer_kernel(
    n_ctx,
    n_exp,
    q_ref,
    k_ref,
    v_ref,
    stream_ref,
    gain_ref,
    ids_ref,
    comb_ref,
    ow_hbm,
    wg_hbm,
    wu_hbm,
    wd_hbm,
    out_ref,
    k_all,
    v_all,
    m_s,
    l_s,
    acc_s,
    att_s,
    ow_v,
    wgu_v,
    wd_v,
    ps_v,
    pr_v,
    mixed_v,
    factor_v,
    pk_v,
    a2_v,
    rows_v,
    h_v,
    part_v,
    sib_v,
    rh0_v,
    rx1_v,
    rh1_v,
    rx0_v,
    ret_v,
    w_sem,
    kv_ss,
    kv_rs,
    kf_ss,
    ps_ss,
    ps_rs,
    a_ss,
    a_rs,
    ag_ss,
    ag_rs,
    rl_ss,
    fw_ss,
    fw_rs,
    sb_ss,
    sb_rs,
    c0_ss,
    c0_rs,
    x1_ss,
    x1_rs,
    c1_ss,
    c1_rs,
    x0_ss,
    x0_rs,
    r_ss,
    r_rs,
):
    c = lax.axis_index("ctx")
    e = lax.axis_index("exp")
    span = q_ref.shape[0]
    heads = q_ref.shape[1] // HD
    toks, dim = stream_ref.shape
    cap = pk_v.shape[1]
    slots = n_exp * cap
    n_chip = n_ctx // 2
    core = lax.rem(c, 2)
    chip = c // 2
    y = c // 4
    xh = lax.rem(chip, 2)
    partner = chip + 1 - 2 * xh
    sibling = chip * 2 + 1 - core
    n_y = n_ctx // 4
    nt = wgu_v.shape[0]
    n_ps = ps_v.shape[0]
    n_p = n_ps
    pw = dim // n_p
    w0 = rh0_v.shape[3] // n_p
    w1 = pw - w0
    g0 = pw * 3 // 8
    g0 = pw * 3 // 8
    far = rows_v.shape[2] - dim

    def extra(p):
        return far if p == n_p - 1 else 0

    def whole_cols(p):
        return pl.ds(p * pw, pw)

    def sent_cols(p):
        return pl.ds(p * pw, pw + extra(p))

    def route_cols(p, h):
        return pl.ds(p * pw, w1) if h else pl.ds(p * pw + w1, w0)

    def sent_route_cols(p, h):
        return pl.ds(p * pw, pw - g0) if h else pl.ds(p * pw + pw - g0, g0 + extra(p))

    def near(p, h):
        return pl.ds(p * w1, w1) if h else pl.ds(p * w0, w0)

    def remote(src, dst, ss, rs, tc, te):
        return pltpu.make_async_remote_copy(
            src_ref=src, dst_ref=dst, send_sem=ss, recv_sem=rs, device_id=(tc, te), device_id_type=MESH
        )

    def weight_copies(n):
        cols = pl.ds(pl.multiple_of(n * HD, HD), HD)
        return (
            pltpu.make_async_copy(wg_hbm.at[:, cols], wgu_v.at[n, :, pl.ds(0, HD)], w_sem.at[0, n]),
            pltpu.make_async_copy(wu_hbm.at[:, cols], wgu_v.at[n, :, pl.ds(HD, HD)], w_sem.at[1, n]),
        )

    ow_copy = pltpu.make_async_copy(ow_hbm, ow_v, w_sem.at[2, 0])
    wd_copy = pltpu.make_async_copy(wd_hbm, wd_v, w_sem.at[2, 1])
    ow_copy.start()

    barrier = pltpu.get_barrier_semaphore()
    pl.semaphore_signal(barrier, inc=1, device_id=(sibling, e), device_id_type=MESH)

    @pl.loop(1, n_chip)
    def _(d):
        tc = lax.rem(chip + d, n_chip) * 2 + core
        pl.semaphore_signal(barrier, inc=1, device_id=(tc, e), device_id_type=MESH)

    @pl.loop(1, n_exp)
    def _(d):
        pl.semaphore_signal(barrier, inc=1, device_id=(c, lax.rem(e + d, n_exp)), device_id_type=MESH)

    pl.semaphore_wait(barrier, n_chip + n_exp - 1)

    def kv_pair(to_chip, block):
        return (
            remote(k_ref, k_all.at[block], kv_ss.at[0, to_chip], kv_rs.at[0, block], to_chip * 2 + core, e),
            remote(v_ref, v_all.at[block], kv_ss.at[1, to_chip], kv_rs.at[1, block], to_chip * 2 + core, e),
        )

    def kv_own():
        return (
            remote(k_ref, k_all.at[c], kf_ss.at[0, chip], kv_rs.at[0, c], sibling, e),
            remote(v_ref, v_all.at[c], kf_ss.at[1, chip], kv_rs.at[1, c], sibling, e),
        )

    def kv_forward(q):
        b = q * 2 + core
        return (
            remote(k_all.at[b], k_all.at[b], kf_ss.at[0, q], kv_rs.at[0, b], sibling, e),
            remote(v_all.at[b], v_all.at[b], kf_ss.at[1, q], kv_rs.at[1, b], sibling, e),
        )

    @pl.when(core == 0)
    def _():
        for cp in kv_own():
            cp.start()

    @pl.loop(chip + 1, n_chip)
    def _(q):
        for cp in kv_pair(q, c):
            cp.start()

    k_all[c] = k_ref[...]
    v_all[c] = v_ref[...]

    @pl.loop(c + 1, y * 4 + 4)
    def _(j):
        k_all[j] = jnp.zeros(k_ref.shape, BF)
        v_all[j] = jnp.zeros(v_ref.shape, BF)

    m_s[...] = jnp.full(m_s.shape, NEG, F32)
    l_s[...] = jnp.zeros(l_s.shape, F32)
    acc_s[...] = jnp.zeros(acc_s.shape, F32)
    scale = 1.0 / math.sqrt(HD)

    def step_off(s):
        return s ^ (s // 2)

    def forward_group(g):
        @pl.loop(g * 2, jnp.minimum(g * 2 + 2, chip))
        def _(q):
            for cp in kv_pair(chip, q * 2 + core):
                cp.wait_recv()
            for cp in kv_forward(q):
                cp.start()

    forward_group(y)

    @pl.loop(0, n_y)
    def _(s):
        g = y - step_off(s)
        g2 = y - step_off(s + 1)

        @pl.when((s < n_y - 1) & (g2 >= 0))
        def _():
            forward_group(g2)

        @pl.when(g >= 0)
        def _():
            @pl.loop(g * 2, jnp.minimum(g * 2 + 2, (c + core) // 2))
            def _(q):
                for cp in kv_pair(chip, q * 2 + 1 - core):
                    cp.wait_recv()

            keys = k_all[pl.ds(g * 4, 4)].reshape(4 * span, HD)
            vals = v_all[pl.ds(g * 4, 4)].reshape(4 * span, HD)
            row = lax.broadcasted_iota(jnp.int32, (span, 4 * span), 0) + (c - g * 4) * span
            col = lax.broadcasted_iota(jnp.int32, (span, 4 * span), 1)
            allowed = row >= col
            for h in range(heads):
                q_h = q_ref[:, h * HD : (h + 1) * HD]
                s_h = lax.dot_general(q_h, keys, NT, preferred_element_type=F32) * scale
                s_h = jnp.where(allowed, s_h, NEG)
                m_old = m_s[h]
                m_new = jnp.maximum(m_old, jnp.max(s_h, axis=1, keepdims=True))
                p = jnp.exp(s_h - m_new[:, :1])
                fix = jnp.exp(m_old - m_new)
                l_s[h] = l_s[h] * fix + jnp.sum(p, axis=1, keepdims=True)
                acc_s[h] = acc_s[h] * fix + jnp.dot(p.astype(BF), vals, preferred_element_type=F32)
                m_s[h] = m_new

    for h in range(heads):
        att_s[:, h * HD : (h + 1) * HD] = (acc_s[h] / l_s[h]).astype(BF)

    ow_copy.wait()

    @pl.loop(0, nt)
    def _(n):
        for cp in weight_copies(n):
            cp.start()

    wd_copy.start()

    def ps_copy(n, te, src_e):
        return remote(ps_v.at[n, te], pr_v.at[n, src_e], ps_ss.at[n, te], ps_rs.at[n, src_e], c, te)

    def project(n):
        r = jnp.dot(att_s[...], ow_v[:, whole_cols(n)], preferred_element_type=F32)
        ps_v[n] = r.reshape(n_exp, toks, pw).astype(BF)

        @pl.loop(1, n_exp)
        def _(d):
            ps_copy(n, lax.rem(e + d, n_exp), e).start()

        pr_v[n, e] = ps_v[n, e]

    project(0)
    project(1)

    slot_row = lax.broadcasted_iota(jnp.int32, (slots, toks), 0)
    slot_exp = slot_row // cap
    first = ids_ref[0:1, :] == slot_exp
    second = ids_ref[1:2, :] == slot_exp
    named = jnp.where(first | second, 1.0, 0.0)
    tri = jnp.where(
        lax.broadcasted_iota(jnp.int32, (toks, toks), 0) < lax.broadcasted_iota(jnp.int32, (toks, toks), 1), 1.0, 0.0
    )
    rank = jnp.dot(named.astype(BF), tri.astype(BF), preferred_element_type=F32)
    slot_rank = (slot_row - slot_exp * cap).astype(F32)
    chosen = jnp.where(rank == slot_rank, named, 0.0)
    chosen_bf = chosen.astype(BF)

    def a_copy(te, src_e, p):
        cols = sent_cols(p)
        return remote(pk_v.at[te, :, cols], a2_v.at[src_e, :, cols], a_ss.at[p, te], a_rs.at[p, src_e], c, te)

    def picked(values):
        r = jnp.dot(chosen_bf, values, preferred_element_type=F32)
        return r.reshape(n_exp, cap, values.shape[1]).astype(BF)

    def dispatch(p, square_sum):
        @pl.loop(1, n_exp)
        def _(d):
            ps_copy(p, e, lax.rem(e + d, n_exp)).wait_recv()

        cols = whole_cols(p)
        mixed = stream_ref[:, cols].astype(F32) + jnp.sum(pr_v[p].astype(F32), axis=0)
        mixed_v[:, cols] = mixed
        square_sum = square_sum + jnp.sum(mixed * mixed, axis=1, keepdims=True)
        pk_v[:, :, cols] = picked((mixed * gain_ref[:, cols]).astype(BF))
        if p == n_p - 1:
            factor = lax.rsqrt(square_sum / dim + 1e-05)
            high = factor.astype(BF).astype(F32)
            middle = (factor - high).astype(BF).astype(F32)
            low = factor - high - middle
            lane = lax.broadcasted_iota(jnp.int32, (toks, far), 1)
            terms = jnp.where(lane == 0, high, jnp.where(lane == 1, middle, jnp.where(lane == 2, low, 0.0)))
            pk_v[:, :, dim : dim + far] = picked(terms.astype(BF))

        @pl.loop(1, n_exp)
        def _(d):
            a_copy(lax.rem(e + d, n_exp), e, p).start()

        a2_v[e, :, sent_cols(p)] = pk_v[e, :, sent_cols(p)]
        return square_sum

    def row_copy(to_chip, q, p, cols, ss, rs):
        part = rows_v.at[q * 2 + core, :, cols]
        return remote(part, part, ss, rs, to_chip * 2 + core, e)

    def own_copy(to_chip, p):
        return row_copy(to_chip, chip, p, sent_cols(p), ag_ss.at[p, to_chip], ag_rs.at[0, p, chip])

    def arrived(q, p):
        row_copy(chip, q, p, sent_cols(p), ag_ss.at[p, chip], ag_rs.at[0, p, q]).wait_recv()

    def arrived_route(q, p, h):
        row_copy(chip, q, p, sent_route_cols(p, h), ag_ss.at[p, chip], ag_rs.at[h, p, q]).wait_recv()

    def relay_y(ty, p):
        return row_copy(ty * 2 + xh, partner, p, sent_route_cols(p, 0), rl_ss.at[0, p, ty], ag_rs.at[0, p, partner])

    def relay_x(yy, p):
        q = yy * 2 + xh
        return row_copy(partner, q, p, sent_route_cols(p, 1), rl_ss.at[1, p, yy], ag_rs.at[1, p, q])

    def fw_copy(q, of_core, p):
        part = rows_v.at[q * 2 + of_core, :, sent_cols(p)]
        return remote(part, part, fw_ss.at[p, q], fw_rs.at[p, q], sibling, e)

    def row_off(s):
        return lax.rem(s, 2) * 2 + s // 2

    def down_y(s):
        return lax.rem(y + n_y - row_off(s), n_y)

    def up_y(s):
        return lax.rem(y + row_off(s), n_y)

    def spread(p):
        @pl.loop(1, n_exp)
        def _(d):
            a_copy(e, lax.rem(e + d, n_exp), p).wait_recv()

        cols = sent_cols(p)
        rows_v[c, :, cols] = a2_v[:, :, cols].astype(F32).reshape(slots, pw + extra(p)).astype(BF)
        own_copy(partner, p).start()

        @pl.loop(1, n_y)
        def _(s):
            own_copy(down_y(s) * 2 + xh, p).start()

        fw_copy(chip, core, p).start()

    def partner_rows(p):
        arrived(partner, p)

        @pl.loop(1, n_y)
        def _(s):
            relay_y(down_y(s), p).start()

        fw_copy(partner, core, p).start()

    def column_rows(s, p):
        q = up_y(s) * 2 + xh
        arrived(q, p)
        relay_x(up_y(s), p).start()
        fw_copy(q, core, p).start()

    def near_rows(p):
        partner_rows(p)

        @pl.loop(1, n_y - 1)
        def _(s):
            column_rows(s, p)

    def other_rows(s, p):
        q = up_y(s) * 2 + 1 - xh
        for h in (0, 1):
            arrived_route(q, p, h)
        fw_copy(q, core, p).start()

    square_sum = jnp.zeros((toks, 1), F32)
    for p in range(n_p):
        square_sum = dispatch(p, square_sum)
        if p + 2 < n_p:
            project(p + 2)
        if p >= 1:
            spread(p - 1)
        if p >= 2:
            near_rows(p - 2)
    spread(n_p - 1)
    near_rows(n_p - 2)
    near_rows(n_p - 1)
    for p in range(n_p - 1):
        column_rows(n_y - 1, p)

    @pl.loop(0, nt)
    def _(n):
        for cp in weight_copies(n):
            cp.wait()

    wd_copy.wait()

    def sb_copy(q, of_core, p):
        cols = whole_cols(p)
        return remote(
            part_v.at[q * 2 + of_core, :, cols], sib_v.at[q, :, cols], sb_ss.at[p, q], sb_rs.at[p, q], sibling, e
        )

    def c0_copy(yy, x2, src_y, p):
        return remote(
            part_v.at[(yy * 2 + x2) * 2 + core, :, route_cols(p, 0)],
            rh0_v.at[src_y, x2, :, near(p, 0)],
            c0_ss.at[p, yy, x2],
            c0_rs.at[p, src_y, x2],
            (yy * 2 + xh) * 2 + core,
            e,
        )

    def x1_copy(yy, p):
        return remote(
            part_v.at[(yy * 2 + 1 - xh) * 2 + core, :, route_cols(p, 1)],
            rx1_v.at[yy, :, near(p, 1)],
            x1_ss.at[p, yy],
            x1_rs.at[p, yy],
            partner * 2 + core,
            e,
        )

    def c1_copy(yy, src_y, p):
        b = (yy * 2 + xh) * 2 + core
        return remote(
            part_v.at[b, :, route_cols(p, 1)],
            rh1_v.at[src_y, :, near(p, 1)],
            c1_ss.at[p, yy],
            c1_rs.at[p, src_y],
            b,
            e,
        )

    def x0_copy(p):
        b = partner * 2 + core
        return remote(
            part_v.at[b, :, route_cols(p, 0)], rx0_v.at[:, near(p, 0)], x0_ss.at[p], x0_rs.at[p], b, e
        )

    def over_cores(yy, p):
        cols = whole_cols(p)
        for x2 in range(2):
            q = yy * 2 + x2
            b = q * 2 + core
            sb_copy(q, core, p).wait_recv()
            part_v[b, :, cols] = (part_v[b, :, cols].astype(F32) + sib_v[q, :, cols].astype(F32)).astype(BF)
        x1_copy(yy, p).start()

        @pl.when(yy != y)
        def _():
            for x2 in range(2):
                c0_copy(yy, x2, y, p).start()

    def over_x(yy, p):
        x1_copy(yy, p).wait_recv()
        b = (yy * 2 + xh) * 2 + core
        cols = route_cols(p, 1)
        part_v[b, :, cols] = (part_v[b, :, cols].astype(F32) + rx1_v[yy, :, near(p, 1)].astype(F32)).astype(BF)

        @pl.when(yy != y)
        def _():
            c1_copy(yy, y, p).start()

    rows_chunk = 4 * slots

    @pl.loop(0, n_y)
    def _(s):
        yy = up_y(s)

        @pl.when(s > 0)
        def _():
            for p in range(n_p):
                over_cores(up_y(s - 1), p)

        @pl.when(s == 1)
        def _():
            for p in range(n_p):
                other_rows(1, p)

        for x2 in range(2):
            for p in range(n_p):
                fw_copy(yy * 2 + x2, 1 - core, p).wait_recv()

        terms = rows_v[pl.ds(yy * 4, 4), :, dim : dim + far].reshape(rows_chunk, far).astype(F32)
        factor_v[...] = jnp.broadcast_to(jnp.sum(terms, axis=1, keepdims=True), (rows_chunk, HD))

        @pl.loop(0, nt)
        def _(n):
            x = rows_v[pl.ds(yy * 4, 4), :, 0:dim].reshape(rows_chunk, dim)
            r = jnp.dot(x, wgu_v[n], preferred_element_type=F32)
            g = r[:, :HD] * factor_v[...]
            u = r[:, HD:] * factor_v[...]
            h_v[:, pl.ds(pl.multiple_of(n * HD, HD), HD)] = (g / (1.0 + jnp.exp(-g)) * u).astype(BF)

        @pl.when(s == 0)
        def _():
            column_rows(n_y - 1, n_p - 1)

        @pl.when((s > 0) & (s < n_y - 1))
        def _():
            for p in range(n_p):
                other_rows(s + 1, p)

        for p in range(n_p):
            o = jnp.dot(h_v[...], wd_v[:, whole_cols(p)], preferred_element_type=F32)
            part_v[pl.ds(yy * 4, 4), :, whole_cols(p)] = o.astype(BF).reshape(4, slots, pw)
            for x2 in range(2):
                sb_copy(yy * 2 + x2, 1 - core, p).start()

        @pl.when((s > 0) & (s < n_y - 1))
        def _():
            for p in range(n_p):
                over_x(up_y(s - 1), p)

    for p in range(n_p):
        over_cores(up_y(n_y - 1), p)
        over_x(up_y(n_y - 2), p)
    for p in range(n_p):
        over_x(up_y(n_y - 1), p)

    def column_sum(b, x2, p):
        total = part_v[b, :, route_cols(p, 0)].astype(F32)
        for d in range(1, n_y):
            total = total + rh0_v[lax.rem(y + d, n_y), x2, :, near(p, 0)].astype(F32)
        return total

    for p in range(n_p):

        @pl.loop(1, n_y)
        def _(d):
            for x2 in range(2):
                c0_copy(y, x2, lax.rem(y + d, n_y), p).wait_recv()

        b = partner * 2 + core
        part_v[b, :, route_cols(p, 0)] = column_sum(b, 1 - xh, p).astype(BF)
        x0_copy(p).start()

    def r_copy(te, src_e, p):
        cols = whole_cols(p)
        return remote(pk_v.at[te, :, cols], ret_v.at[src_e, :, cols], r_ss.at[p, te], r_rs.at[p, src_e], c, te)

    for p in range(n_p):

        @pl.loop(1, n_exp)
        def _(d):
            a_copy(lax.rem(e + d, n_exp), e, p).wait_send()

        @pl.loop(1, n_y)
        def _(d):
            c1_copy(y, lax.rem(y + d, n_y), p).wait_recv()

        total = part_v[c, :, route_cols(p, 1)].astype(F32)
        for d in range(1, n_y):
            total = total + rh1_v[lax.rem(y + d, n_y), :, near(p, 1)].astype(F32)
        pk_v[:, :, route_cols(p, 1)] = total.reshape(n_exp, cap, w1).astype(BF)
        x0_copy(p).wait_recv()
        total = column_sum(c, xh, p) + rx0_v[:, near(p, 0)].astype(F32)
        pk_v[:, :, route_cols(p, 0)] = total.reshape(n_exp, cap, w0).astype(BF)

        @pl.loop(1, n_exp)
        def _(d):
            r_copy(lax.rem(e + d, n_exp), e, p).start()

        ret_v[e, :, whole_cols(p)] = pk_v[e, :, whole_cols(p)]

    wt = chosen * jnp.where(first, comb_ref[0:1, :], comb_ref[1:2, :])
    w_hi = wt.astype(BF)
    w_lo = (wt - w_hi.astype(F32)).astype(BF)

    for p in range(n_p):

        @pl.loop(1, n_exp)
        def _(d):
            r_copy(e, lax.rem(e + d, n_exp), p).wait_recv()

        cols = whole_cols(p)
        r = ret_v[:, :, cols].astype(F32).reshape(slots, pw).astype(BF)
        o = lax.dot_general(w_hi, r, TN, preferred_element_type=F32)
        o = o + lax.dot_general(w_lo, r, TN, preferred_element_type=F32)
        out_ref[:, cols] = (mixed_v[:, cols] + o).astype(BF)

    @pl.when(core == 0)
    def _():
        for cp in kv_own():
            cp.wait_send()

    @pl.loop(chip + 1, n_chip)
    def _(q):
        for cp in kv_pair(q, c):
            cp.wait_send()

    @pl.loop(0, chip)
    def _(q):
        for cp in kv_forward(q):
            cp.wait_send()

    for p in range(n_p):

        @pl.loop(1, n_exp)
        def _(d):
            te = lax.rem(e + d, n_exp)
            ps_copy(p, te, e).wait_send()
            r_copy(te, e, p).wait_send()

        own_copy(partner, p).wait_send()
        x0_copy(p).wait_send()

        @pl.loop(0, n_chip)
        def _(q):
            fw_copy(q, core, p).wait_send()
            sb_copy(q, 1 - core, p).wait_send()

        @pl.loop(1, n_y)
        def _(s):
            yy = up_y(s)
            own_copy(yy * 2 + xh, p).wait_send()
            relay_y(yy, p).wait_send()
            relay_x(yy, p).wait_send()
            for x2 in range(2):
                c0_copy(yy, x2, y, p).wait_send()
            c1_copy(yy, y, p).wait_send()

        @pl.loop(0, n_y)
        def _(yy):
            x1_copy(yy, p).wait_send()


def body(
    stream, queries, attn_keys, attn_values, out_weight, norm_gain, expert_ids, combine, w_gate, w_up, w_down
):
    n_ctx = lax.axis_size("ctx")
    n_exp = lax.axis_size("exp")
    span, qw = queries.shape
    toks, dim = stream.shape
    hid = w_gate.shape[2]
    heads = qw // HD
    cap = toks // 2
    slots = n_exp * cap
    n_chip = n_ctx // 2
    nt = hid // HD
    n_ps = 4
    n_y = n_ctx // 4
    w0 = dim * 2 // 8
    vm = pl.BlockSpec(memory_space=pltpu.VMEM)
    hbm = pl.BlockSpec(memory_space=pl.ANY)
    dma = pltpu.SemaphoreType.DMA
    scratch = [
        pltpu.VMEM((n_ctx, span, HD), BF),
        pltpu.VMEM((n_ctx, span, HD), BF),
        pltpu.VMEM((heads, span, HD), F32),
        pltpu.VMEM((heads, span, HD), F32),
        pltpu.VMEM((heads, span, HD), F32),
        pltpu.VMEM((span, qw), BF),
        pltpu.VMEM((qw, dim), BF),
        pltpu.VMEM((nt, dim, 2 * HD), BF),
        pltpu.VMEM((hid, dim), BF),
        pltpu.VMEM((n_ps, n_exp, toks, dim // n_ps), BF),
        pltpu.VMEM((n_ps, n_exp, toks, dim // n_ps), BF),
        pltpu.VMEM((toks, dim), F32),
        pltpu.VMEM((4 * slots, HD), F32),
        pltpu.VMEM((n_exp, cap, dim + HD), BF),
        pltpu.VMEM((n_exp, cap, dim + HD), BF),
        pltpu.VMEM((n_ctx, slots, dim + HD), BF),
        pltpu.VMEM((4 * slots, hid), BF),
        pltpu.VMEM((n_ctx, slots, dim), BF),
        pltpu.VMEM((n_chip, slots, dim), BF),
        pltpu.VMEM((n_y, 2, slots, w0), BF),
        pltpu.VMEM((n_y, slots, dim - w0), BF),
        pltpu.VMEM((n_y, slots, dim - w0), BF),
        pltpu.VMEM((slots, w0), BF),
        pltpu.VMEM((n_exp, cap, dim), BF),
        dma((3, nt)),
        dma((2, n_chip)),
        dma((2, n_ctx)),
        dma((2, n_chip)),
        dma((n_ps, n_exp)),
        dma((n_ps, n_exp)),
        dma((n_ps, n_exp)),
        dma((n_ps, n_exp)),
        dma((n_ps, n_chip)),
        dma((2, n_ps, n_chip)),
        dma((2, n_ps, n_y)),
        dma((n_ps, n_chip)),
        dma((n_ps, n_chip)),
        dma((n_ps, n_chip)),
        dma((n_ps, n_chip)),
        dma((n_ps, n_y, 2)),
        dma((n_ps, n_y, 2)),
        dma((n_ps, n_y)),
        dma((n_ps, n_y)),
        dma((n_ps, n_y)),
        dma((n_ps, n_y)),
        dma((n_ps,)),
        dma((n_ps,)),
        dma((n_ps, n_exp)),
        dma((n_ps, n_exp)),
    ]
    return pl.pallas_call(
        functools.partial(layer_kernel, n_ctx, n_exp),
        out_shape=jax.ShapeDtypeStruct((toks, dim), BF),
        in_specs=[vm] * 7 + [hbm] * 4,
        out_specs=vm,
        scratch_shapes=scratch,
        compiler_params=pltpu.CompilerParams(
            collective_id=0, has_side_effects=True, vmem_limit_bytes=67_000_000
        ),
        name="decoder_layer",
    )(
        queries,
        attn_keys,
        attn_values,
        stream,
        norm_gain.reshape(1, dim),
        expert_ids.T,
        combine.T,
        out_weight,
        w_gate[0],
        w_up[0],
        w_down[0],
    )


def solution(mesh):
    in_specs = (
        P(("ctx", "exp"), None),
        P("ctx", "exp"),
        P("ctx", "exp"),
        P("ctx", "exp"),
        P("exp", None),
        P(),
        P(("ctx", "exp"), None),
        P(("ctx", "exp"), None),
        P("exp", None, "ctx"),
        P("exp", None, "ctx"),
        P("exp", "ctx", None),
    )
    out_specs = P(("ctx", "exp"), None)
    return jax.shard_map(body, mesh=mesh, in_specs=in_specs, out_specs=out_specs, check_vma=False)
```
